32 devices in a mesh: row: 8 (over y, x, core), col: 4 (over z).
Axes of the slice: x: 2, y: 2, z: 4, core: 2. Of those that a mesh axis runs over, the one named last changes fastest.
Arguments:
- start_modes: float32 [32, 131072], P(None, ('row', 'col')), may hold values from -6 to 6
- energies: float32 [131072], P(('row', 'col')), may hold values from -0.5 to 0.5
- coupling: float32 [2048, 20, 4096], P('row', 'col'), may hold values from -0.078125 to 0.078125
- pattern: int32 [2048, 20], P('row', 'col'), may hold values from 0 to 2047, as said below
Outputs:
- filtered: float32 [32, 131072], P(None, ('row', 'col'))
- previous: float32 [32, 131072], P(None, ('row', 'col'))
The draws below stay inside these ranges and needn't reach their ends.
Inputs may be any that keep to these rules, and one draw needn't show every extreme that they name: In block row i, the 5 entries pattern[i, c * 5] to pattern[i, c * 5 + 4] are distinct block columns j with (j // 64) % 4 == c.
All inputs are finite; a program needn't handle non-finite values.
Results may differ from the reference program's by a relative error of at most 0.0001.
Values sent between devices are 32-bit elements; how exact they have to be, the bound alone decides.
A program may use at most 192 MiB of HBM per device.

```python
import jax
import jax.numpy as jnp
from jax import lax

BASIS = 131072
BLOCK = 64
SLOTS = 5
MODES = 32
DEGREE = 3
BLOCKS = 2048
COUPLED = 20
N_ROW = 8
N_COL = 4


def draw_pattern(key, part):
    block_count = BASIS // BLOCK
    group_size = block_count // N_COL
    per_piece = block_count // (N_ROW * N_COL)
    stride = group_size // SLOTS
    key_jitter, key_rotate = jax.random.split(key)
    jitter = jax.random.randint(key_jitter, (block_count, N_COL, SLOTS), 0, stride)
    rotate = jax.random.randint(key_rotate, (block_count, N_COL, 1), 0, group_size)
    offsets = (jnp.arange(SLOTS, dtype=jnp.int32)[None, None, :] * stride + jitter + rotate) % group_size
    piece_row = offsets // per_piece
    within = offsets % per_piece
    column = jnp.arange(N_COL, dtype=jnp.int32)[None, :, None]
    return ((piece_row * N_COL + column) * per_piece + within).reshape(block_count, N_COL * SLOTS).astype(jnp.int32)


def block_scale(key, shape, pieces, low, high):
    gain, own = 1.0, jax.random.fold_in(key, 6)
    for dim, parts in pieces:
        steps = jnp.exp(jax.random.uniform(jax.random.fold_in(own, dim), (parts,), jnp.float32, low / len(pieces), high / len(pieces)))
        gain = gain * jnp.repeat(steps, shape[dim] // parts).reshape([-1 if axis == dim else 1 for axis in range(len(shape))])
    return gain


def bell_draw(key, dims, deviation, reach, cuts=(), kind=jnp.bfloat16):
    values = jax.random.normal(key, dims, jnp.float32) * deviation
    if len(cuts) > 0:
        values = block_scale(key, dims, cuts, -0.22, 0.18) * values
    return jnp.clip(values, min=-reach, max=reach).astype(kind)


def setup_inputs(seed: int = 0) -> dict:
    keys = jax.random.split(jax.random.key(seed), 5)
    start_modes = bell_draw(keys[0], (MODES, BASIS), 1.0, 6.0, ((1, 32),), jnp.float32)
    energies = jnp.clip(jax.random.uniform(keys[1], (BASIS,), jnp.float32, -0.5, 0.5) * block_scale(keys[1], (BASIS,), ((0, 32),), -0.4, 0.0), -0.5, 0.5)
    coupling = bell_draw(keys[2], (BLOCKS, COUPLED, BLOCK * BLOCK), (4 * BLOCK * COUPLED) ** -0.5, 0.078125, ((0, 8), (1, 4)), jnp.float32)
    pattern = draw_pattern(jax.random.fold_in(keys[4], 71), 0)
    return {"start_modes": start_modes, "energies": energies, "coupling": coupling, "pattern": pattern}


def operate(vector, energies, coupling, pattern):
    mode_count = vector.shape[0]
    blocks = vector.reshape(mode_count, BLOCKS, BLOCK)
    group_rows = min(BLOCKS, 128)
    groups = BLOCKS // group_rows

    def block_rows(inputs):
        sub_mats, sub_cols = inputs
        picked = jnp.take(blocks, sub_cols.reshape(-1), axis=1).reshape(mode_count, group_rows, COUPLED, BLOCK)
        block_mats = sub_mats.reshape(group_rows, COUPLED, BLOCK, BLOCK)
        return jnp.einsum("mrsb,rsab->rma", picked, block_mats, precision=lax.Precision.HIGHEST)

    result = lax.map(block_rows, (coupling.reshape(groups, group_rows, COUPLED, BLOCK * BLOCK), pattern.reshape(groups, group_rows, COUPLED)))
    coupled = jnp.transpose(result, (2, 0, 1, 3)).reshape(mode_count, BASIS)
    return energies[None, :] * vector + coupled


def reference(start_modes, energies, coupling, pattern):
    previous = start_modes
    current = operate(start_modes, energies, coupling, pattern)
    for degree in range(DEGREE - 1):
        upcoming = 2.0 * operate(current, energies, coupling, pattern) - previous
        previous = current
        current = upcoming
    return current, previous
```

```python
import functools

import jax
import jax.numpy as jnp
from jax import lax
from jax.experimental import pallas as pl
from jax.experimental.pallas import tpu as pltpu
from jax.sharding import PartitionSpec as P

BLOCK = 64
DEGREE = 3
LANES = 128
SUBLANES = 8


def low_half(shape):
    return lax.broadcasted_iota(jnp.int32, shape, len(shape) - 1) < BLOCK


def split(x):
    high = x.astype(jnp.bfloat16)
    return high, (x - high.astype(jnp.float32)).astype(jnp.bfloat16)


MESH = pl.DeviceIdType.MESH


def filter_kernel(
    slots, n_row, n_col, halves,
    places_ref, start_ref, energies_ref, coupling_ref, filtered_ref, previous_ref,
    raw, prepared, gathered, blocks, first_ref, partial, landed,
    raw_sem, gather_send, gather_recv, share_send, share_recv,
):
    row, col = lax.axis_index("row"), lax.axis_index("col")
    chips = n_row // 2
    chip, core = row // 2, row % 2
    partner = chip * 2 + (1 - core)
    modes, piece_len = start_ref.shape
    part = modes // halves
    tiles = piece_len // LANES
    per_piece = piece_len // BLOCK
    rows = prepared.shape[0]
    group = min(16, per_piece)
    pairs = (slots + 1) // 2
    terms = (start_ref, first_ref, previous_ref, filtered_ref)
    relay = chips == 4

    def other_chip(d):
        if chips & (chips - 1):
            return (chip + d) % chips
        place, bit, rest = chip, 1, abs(d)
        while rest:
            if rest % 2:
                place = place + bit * (1 - 2 * (chip // bit % 2))
            bit, rest = 2 * bit, rest // 2
        return place

    def same_core(d):
        return other_chip(d) * 2 + core

    def other_core(d):
        return other_chip(d) * 2 + (1 - core)

    def share_of(k, h):
        return terms[k].at[pl.ds(h * part, part), :]

    barrier = pltpu.get_barrier_semaphore()
    for d in range(1, chips):
        pl.semaphore_signal(barrier, inc=1, device_id=(same_core(d), col), device_id_type=MESH)
    pl.semaphore_signal(barrier, inc=1, device_id=(partner, col), device_id_type=MESH)
    for d in (1, n_col - 1):
        pl.semaphore_signal(barrier, inc=1, device_id=(row, (col + d) % n_col), device_id_type=MESH)
    pl.semaphore_wait(barrier, chips + 2)

    def gather_copy(k, h, source, slot, send, recv, target, modes_of=None):
        place = gathered.at[k, h, slot] if modes_of is None else gathered.at[k, h, slot, modes_of, :]
        return pltpu.make_async_remote_copy(
            src_ref=source,
            dst_ref=place,
            send_sem=gather_send.at[k, h, send],
            recv_sem=gather_recv.at[k, h, recv],
            device_id=(target, col),
            device_id_type=MESH,
        )

    def own_copies(k, h):
        source = share_of(k, h)
        reach = range(1, 3) if relay else range(1, chips)
        return [gather_copy(k, h, source, row, d, row, same_core(d)) for d in reach] + [
            gather_copy(k, h, source, row, 0, row, partner)
        ]

    def passed_copy(k, h, d):
        slot = same_core(-d)
        return gather_copy(k, h, gathered.at[k, h, slot], slot, chips + d, slot, partner)

    def relay_copy(k, h, d):
        slot, which = same_core(d), pl.ds((d - 1) * (part // 2), part // 2)
        source = gathered.at[k, h, slot, which, :]
        recv = slot if d == 1 else n_row
        return gather_copy(k, h, source, slot, 3 if d == 1 else chips, recv, same_core(3 - d), which)

    def relay_arrival(k, h, d):
        slot, which = same_core(3), pl.ds((d - 1) * (part // 2), part // 2)
        place = gathered.at[k, h, slot, which, :]
        return gather_copy(k, h, place, slot, 0, slot if d == 1 else n_row, partner, which)

    def arrival(k, h, slot):
        return gather_copy(k, h, gathered.at[k, h, slot], slot, 0, slot, partner)

    def gather_start(k, h):
        for copy in own_copies(k, h):
            copy.start()

    def gather_pass(k, h):
        if relay:
            for d in range(1, 3):
                arrival(k, h, same_core(d)).wait_recv()
                relay_copy(k, h, d).start()
                passed_copy(k, h, d).start()

    def gather_finish(k, h):
        if relay:
            for d in range(1, 3):
                relay_arrival(k, h, d).wait_recv()
            passed_copy(k, h, 3).start()
        else:
            for d in range(1, chips):
                arrival(k, h, same_core(-d)).wait_recv()
                passed_copy(k, h, d).start()
        arrival(k, h, partner).wait_recv()
        for d in range(1, chips):
            arrival(k, h, other_core(-d)).wait_recv()

    def target_of(d):
        above, below = n_col - 1 - col, col
        lower = jnp.where(d < above, n_col - 1 - d, d - above)
        upper = jnp.where(d < below, d, n_col - 1 - (d - below))
        return jnp.where(2 * col < n_col, lower, upper)

    def share_copy(k, h, target):
        to = jnp.where(target > col, col + 1, col - 1)
        slot = jnp.where((target < col) & (to == target), n_col, target)
        return pltpu.make_async_remote_copy(
            src_ref=partial.at[k, h, target],
            dst_ref=landed.at[k, h, slot],
            send_sem=share_send.at[k, h, target],
            recv_sem=share_recv.at[k, h, slot],
            device_id=(row, to),
            device_id_type=MESH,
        )

    def share_arrival(k, h, slot):
        return pltpu.make_async_remote_copy(
            src_ref=partial.at[k, h, 0],
            dst_ref=landed.at[k, h, slot],
            send_sem=share_send.at[k, h, 0],
            recv_sem=share_recv.at[k, h, slot],
            device_id=(row, (col + 1) % n_col),
            device_id_type=MESH,
        )

    wide = min(piece_len, 4 * LANES)

    def add_landed(k, h, target, slot):
        def some(t, carry):
            at = pl.ds(pl.multiple_of(t * wide, wide), wide)
            partial[k, h, target, :, at] = partial[k, h, target, :, at] + landed[k, h, slot, :, at]
            return carry

        lax.fori_loop(0, piece_len // wide, some, 0)

    def at_the_end(target):
        return jnp.where(target > col, col == 0, col == n_col - 1)

    def forward(k, h, d):
        target = target_of(d)

        @pl.when(jnp.logical_not(at_the_end(target)))
        def _():
            share_arrival(k, h, target).wait_recv()
            add_landed(k, h, target, target)
            share_copy(k, h, target).start()

    def forward_some(k, h, first, last):
        def one(d, carry):
            forward(k, h, d)
            return carry

        lax.fori_loop(first, last, one, 0)

    chunk = raw.shape[2] * SUBLANES
    chunks = rows // chunk

    def fetch(index, slot):
        first = pl.multiple_of(index * (chunk // SUBLANES), chunk // SUBLANES)
        return [
            pltpu.make_async_copy(
                coupling_ref.at[s, pl.ds(first, chunk // SUBLANES), :, i, :],
                raw.at[slot, s, :, i],
                raw_sem.at[slot, s, i],
            )
            for s in range(slots)
            for i in range(SUBLANES)
        ]

    def prepare_chunk(index, carry):
        slot = index % 2

        @pl.when(index + 1 < chunks)
        def _():
            for copy in fetch(index + 1, 1 - slot):
                copy.start()

        for copy in fetch(index, slot):
            copy.wait()
        low = low_half((BLOCK // 2, LANES))

        def eight(j, carry):
            for i in range(SUBLANES):
                at = index * chunk + j * SUBLANES + i
                for q in range(pairs):
                    one = raw[slot, 2 * q, j, i]
                    one_turned = pltpu.roll(one, BLOCK, 1)
                    if 2 * q + 1 < slots:
                        two = raw[slot, 2 * q + 1, j, i]
                        two_turned = pltpu.roll(two, BLOCK, 1)
                    else:
                        two = two_turned = jnp.zeros_like(one)
                    both = jnp.concatenate([jnp.where(low, one, two_turned), jnp.where(low, one_turned, two)], axis=0)
                    high, rest = split(both)
                    prepared[at, :BLOCK, q * LANES : (q + 1) * LANES] = high
                    prepared[at, BLOCK:, q * LANES : (q + 1) * LANES] = rest
            return carry

        lax.fori_loop(0, chunk // SUBLANES, eight, 0)
        return carry

    def fill(k, h):
        low = low_half((part, LANES))

        def one(index, carry):
            for t in range(tiles):
                x = gathered[k, h, index, :, t * LANES : (t + 1) * LANES]
                turned = pltpu.roll(x, BLOCK, 1)
                for side, value in enumerate((jnp.where(low, x, turned), jnp.where(low, turned, x))):
                    high, rest = split(value)
                    place = index * (2 * tiles) + 2 * t + side
                    blocks[place, :part, :] = high
                    blocks[place, part:, :] = rest
            return carry

        lax.fori_loop(0, n_row, one, 0)

    def compute(k, h, first, last):
        low = low_half((part, LANES))
        low_picked = low_half((2 * part, LANES))

        def one_part(d, carry):
            target = target_of(d)

            def some_rows(step, carry):
                at = target * per_piece + step * group
                done = []
                for i in range(group):
                    base = (at + i) * slots
                    picked = [blocks[places_ref[base + s]] for s in range(slots)]
                    sides = [
                        jnp.where(low_picked, picked[2 * q], picked[2 * q + 1]) if 2 * q + 1 < slots else picked[2 * q]
                        for q in range(pairs)
                    ]
                    product = lax.dot_general(
                        jnp.concatenate(sides, axis=1),
                        prepared[at + i],
                        (((1,), (1,)), ((), ())),
                        preferred_element_type=jnp.float32,
                    )
                    total = product[:part] + product[part:]
                    done.append(total + pltpu.roll(total, BLOCK, 1))
                width = group * BLOCK
                joined = [jnp.where(low, done[2 * q], done[2 * q + 1]) for q in range(group // 2)]
                partial[k, h, target, :, pl.ds(pl.multiple_of(step * width, width), width)] = jnp.concatenate(joined, axis=1)
                return carry

            lax.fori_loop(0, per_piece // group, some_rows, 0)

            @pl.when((target != col) & at_the_end(target))
            def _():
                share_copy(k, h, target).start()

            return carry

        lax.fori_loop(first, last, one_part, 0)

    def update(k, h):
        @pl.when(col > 0)
        def _():
            share_arrival(k, h, col).wait_recv()
            add_landed(k, h, col, col)

        @pl.when(col < n_col - 1)
        def _():
            share_arrival(k, h, n_col).wait_recv()
            add_landed(k, h, col, n_col)

        here = slice(h * part, (h + 1) * part)
        lane = lax.broadcasted_iota(jnp.int32, (part, LANES), 1)
        order = lane // BLOCK * BLOCK + lane % 2 * (BLOCK // 2) + lane % BLOCK // 2

        def tile(t, carry):
            at = pl.ds(pl.multiple_of(t * LANES, LANES), LANES)
            total = jnp.take_along_axis(partial[k, h, col, :, at], order, axis=1)
            total = energies_ref[:, at] * terms[k][here, at] + total
            if k > 0:
                total = 2.0 * total - terms[k - 1][here, at]
            terms[k + 1][here, at] = total
            if k + 1 < DEGREE:
                gathered[k + 1, h, row, :, at] = total
            return carry

        lax.fori_loop(0, tiles, tile, 0)

    stages = [(k, h) for k in range(DEGREE) for h in range(halves)]
    early = n_col // 2
    soon = max(n_col - 3, 0)

    for copy in fetch(0, 0):
        copy.start()
    gather_start(0, 0)
    for h in range(halves):
        gathered[0, h, row] = share_of(0, h)[...]
    lax.fori_loop(0, chunks // 2, prepare_chunk, 0)
    gather_pass(0, 0)
    for h in range(1, halves):
        gather_start(0, h)
    lax.fori_loop(chunks // 2, chunks, prepare_chunk, 0)
    gather_finish(0, 0)
    fill(0, 0)

    for index, (k, h) in enumerate(stages):
        later = stages[index + 1] if index + 1 < len(stages) else None
        compute(k, h, 0, early)
        if index > 0:
            update(*stages[index - 1])
            if later is not None and later[0] > 0:
                gather_start(*later)
        compute(k, h, early, n_col - 1)
        forward_some(k, h, 0, soon)
        compute(k, h, n_col - 1, n_col)
        if later is not None:
            gather_pass(*later)
        forward_some(k, h, soon, n_col - 1)
        if later is not None:
            gather_finish(*later)
            fill(*later)
    update(*stages[-1])

    for k in range(DEGREE):
        for h in range(halves):
            for copy in own_copies(k, h) + [passed_copy(k, h, d) for d in range(1, chips)]:
                copy.wait_send()
            if relay:
                for d in range(1, 3):
                    relay_copy(k, h, d).wait_send()

            def one(d, carry):
                share_copy(k, h, target_of(d)).wait_send()
                return carry

            lax.fori_loop(0, n_col - 1, one, 0)


def shards(start_modes, energies, coupling, pattern):
    n_row, n_col = lax.axis_size("row"), lax.axis_size("col")
    modes, piece_len = start_modes.shape
    per_piece = piece_len // BLOCK
    rows, slots, entries = coupling.shape
    pairs = (slots + 1) // 2
    chunk, halves = 32, 2
    part = modes // halves
    tall = entries // LANES
    places = (pattern // per_piece // n_col * per_piece + pattern % per_piece).reshape(-1)
    by_slot = jnp.transpose(coupling, (1, 0, 2)).reshape(slots, rows // SUBLANES, SUBLANES, tall, LANES)
    vmem = pl.BlockSpec(memory_space=pltpu.VMEM)
    filtered, previous = pl.pallas_call(
        functools.partial(filter_kernel, slots, n_row, n_col, halves),
        in_specs=[pl.BlockSpec(memory_space=pltpu.SMEM), vmem, vmem, pl.BlockSpec(memory_space=pl.ANY)],
        out_specs=[vmem, vmem],
        out_shape=[jax.ShapeDtypeStruct(start_modes.shape, jnp.float32)] * 2,
        scratch_shapes=[
            pltpu.VMEM((2, slots, chunk // SUBLANES, SUBLANES, tall, LANES), jnp.float32),
            pltpu.VMEM((rows, 2 * BLOCK, pairs * LANES), jnp.bfloat16),
            pltpu.VMEM((DEGREE, halves, n_row, part, piece_len), jnp.float32),
            pltpu.VMEM((n_row * per_piece, 2 * part, LANES), jnp.bfloat16),
            pltpu.VMEM((modes, piece_len), jnp.float32),
            pltpu.VMEM((DEGREE, halves, n_col, part, piece_len), jnp.float32),
            pltpu.VMEM((DEGREE, halves, n_col + 1, part, piece_len), jnp.float32),
            pltpu.SemaphoreType.DMA((2, slots, SUBLANES)),
            pltpu.SemaphoreType.DMA((DEGREE, halves, n_row)),
            pltpu.SemaphoreType.DMA((DEGREE, halves, n_row + 1)),
            pltpu.SemaphoreType.DMA((DEGREE, halves, n_col)),
            pltpu.SemaphoreType.DMA((DEGREE, halves, n_col + 1)),
        ],
        compiler_params=pltpu.CompilerParams(collective_id=0, has_side_effects=True, vmem_limit_bytes=67043328),
        name="filter",
    )(places, start_modes, energies.reshape(1, -1), jnp.transpose(by_slot, (0, 1, 3, 2, 4)))
    return filtered, previous


def solution(mesh):
    in_specs = (P(None, ("row", "col")), P(("row", "col")), P("row", "col", None), P("row", "col"))
    out_specs = (P(None, ("row", "col")), P(None, ("row", "col")))
    return jax.shard_map(shards, mesh=mesh, in_specs=in_specs, out_specs=out_specs, check_vma=False)
```

```python
import functools

import jax
import jax.numpy as jnp
from jax import lax
from jax.experimental import pallas as pl
from jax.experimental.pallas import tpu as pltpu
from jax.sharding import PartitionSpec as P

BLOCK = 64
DEGREE = 3
LANES = 128
SUBLANES = 8


def low_half(shape):
    return lax.broadcasted_iota(jnp.int32, shape, len(shape) - 1) < BLOCK


def split(x):
    high = x.astype(jnp.bfloat16)
    return high, (x - high.astype(jnp.float32)).astype(jnp.bfloat16)


MESH = pl.DeviceIdType.MESH


def filter_kernel(
    slots, n_row, n_col, halves,
    places_ref, start_ref, energies_ref, coupling_ref, filtered_ref, previous_ref,
    raw, prepared, gathered, blocks, first_ref, partial, landed,
    raw_sem, gather_send, gather_recv, share_send, share_recv,
):
    row, col = lax.axis_index("row"), lax.axis_index("col")
    chips = n_row // 2
    chip, core = row // 2, row % 2
    partner = chip * 2 + (1 - core)
    modes, piece_len = start_ref.shape
    part = modes // halves
    tiles = piece_len // LANES
    per_piece = piece_len // BLOCK
    rows = prepared.shape[0]
    group = min(16, per_piece)
    pairs = (slots + 1) // 2
    terms = (start_ref, first_ref, previous_ref, filtered_ref)
    relay = chips == 4

    def other_chip(d):
        if chips & (chips - 1):
            return (chip + d) % chips
        place, bit, rest = chip, 1, abs(d)
        while rest:
            if rest % 2:
                place = place + bit * (1 - 2 * (chip // bit % 2))
            bit, rest = 2 * bit, rest // 2
        return place

    def same_core(d):
        return other_chip(d) * 2 + core

    def other_core(d):
        return other_chip(d) * 2 + (1 - core)

    def share_of(k, h):
        return terms[k].at[pl.ds(h * part, part), :]

    barrier = pltpu.get_barrier_semaphore()
    for d in range(1, chips):
        pl.semaphore_signal(barrier, inc=1, device_id=(same_core(d), col), device_id_type=MESH)
    pl.semaphore_signal(barrier, inc=1, device_id=(partner, col), device_id_type=MESH)
    for d in (1, n_col - 1):
        pl.semaphore_signal(barrier, inc=1, device_id=(row, (col + d) % n_col), device_id_type=MESH)
    pl.semaphore_wait(barrier, chips + 2)

    def gather_copy(k, h, source, slot, send, recv, target, modes_of=None):
        place = gathered.at[k, h, slot] if modes_of is None else gathered.at[k, h, slot, modes_of, :]
        return pltpu.make_async_remote_copy(
            src_ref=source,
            dst_ref=place,
            send_sem=gather_send.at[k, h, send],
            recv_sem=gather_recv.at[k, h, recv],
            device_id=(target, col),
            device_id_type=MESH,
        )

    def own_copies(k, h):
        source = share_of(k, h)
        reach = range(1, 3) if relay else range(1, chips)
        return [gather_copy(k, h, source, row, d, row, same_core(d)) for d in reach] + [
            gather_copy(k, h, source, row, 0, row, partner)
        ]

    def passed_copy(k, h, d):
        slot = same_core(-d)
        return gather_copy(k, h, gathered.at[k, h, slot], slot, chips + d, slot, partner)

    def relay_copy(k, h, d):
        slot, which = same_core(d), pl.ds((d - 1) * (part // 2), part // 2)
        source = gathered.at[k, h, slot, which, :]
        recv = slot if d == 1 else n_row
        return gather_copy(k, h, source, slot, 3 if d == 1 else chips, recv, same_core(3 - d), which)

    def relay_arrival(k, h, d):
        slot, which = same_core(3), pl.ds((d - 1) * (part // 2), part // 2)
        place = gathered.at[k, h, slot, which, :]
        return gather_copy(k, h, place, slot, 0, slot if d == 1 else n_row, partner, which)

    def arrival(k, h, slot):
        return gather_copy(k, h, gathered.at[k, h, slot], slot, 0, slot, partner)

    def gather_start(k, h):
        for copy in own_copies(k, h):
            copy.start()

    near = range(1, 3) if relay else range(1, chips)

    def gather_pass(k, h):
        for d in near:
            arrival(k, h, same_core(-d)).wait_recv()
            if relay:
                relay_copy(k, h, d).start()
            passed_copy(k, h, d).start()
        fill(k, h, [row] + [same_core(-d) for d in near])

    def gather_finish(k, h):
        arrival(k, h, partner).wait_recv()
        for d in near:
            arrival(k, h, other_core(-d)).wait_recv()
        fill(k, h, [partner] + [other_core(-d) for d in near])
        if relay:
            for d in range(1, 3):
                relay_arrival(k, h, d).wait_recv()
            passed_copy(k, h, 3).start()
            arrival(k, h, other_core(3)).wait_recv()
            fill(k, h, [same_core(3), other_core(3)])

    def target_of(d):
        above, below = n_col - 1 - col, col
        lower = jnp.where(d < above, n_col - 1 - d, d - above)
        upper = jnp.where(d < below, d, n_col - 1 - (d - below))
        return jnp.where(2 * col < n_col, lower, upper)

    def share_copy(k, h, target):
        to = jnp.where(target > col, col + 1, col - 1)
        slot = jnp.where((target < col) & (to == target), n_col, target)
        return pltpu.make_async_remote_copy(
            src_ref=partial.at[k, h, target],
            dst_ref=landed.at[k, h, slot],
            send_sem=share_send.at[k, h, target],
            recv_sem=share_recv.at[k, h, slot],
            device_id=(row, to),
            device_id_type=MESH,
        )

    def share_arrival(k, h, slot):
        return pltpu.make_async_remote_copy(
            src_ref=partial.at[k, h, 0],
            dst_ref=landed.at[k, h, slot],
            send_sem=share_send.at[k, h, 0],
            recv_sem=share_recv.at[k, h, slot],
            device_id=(row, (col + 1) % n_col),
            device_id_type=MESH,
        )

    wide = min(piece_len, 8 * LANES)

    def add_landed(k, h, target, slot):
        def some(t, carry):
            at = pl.ds(pl.multiple_of(t * wide, wide), wide)
            partial[k, h, target, :, at] = partial[k, h, target, :, at] + landed[k, h, slot, :, at]
            return carry

        lax.fori_loop(0, piece_len // wide, some, 0)

    def at_the_end(target):
        return jnp.where(target > col, col == 0, col == n_col - 1)

    def forward(k, h, d):
        target = target_of(d)

        @pl.when(jnp.logical_not(at_the_end(target)))
        def _():
            share_arrival(k, h, target).wait_recv()
            add_landed(k, h, target, target)
            share_copy(k, h, target).start()

    def forward_some(k, h, first, last):
        def one(d, carry):
            forward(k, h, d)
            return carry

        lax.fori_loop(first, last, one, 0)

    chunk = raw.shape[2] * SUBLANES
    chunks = rows // chunk

    def fetch(index, slot):
        first = pl.multiple_of(index * (chunk // SUBLANES), chunk // SUBLANES)
        return [
            pltpu.make_async_copy(
                coupling_ref.at[s, pl.ds(first, chunk // SUBLANES), :, i, :],
                raw.at[slot, s, :, i],
                raw_sem.at[slot, s, i],
            )
            for s in range(slots)
            for i in range(SUBLANES)
        ]

    def prepare_chunk(index, carry):
        slot = index % 2

        @pl.when(index + 1 < chunks)
        def _():
            for copy in fetch(index + 1, 1 - slot):
                copy.start()

        for copy in fetch(index, slot):
            copy.wait()
        low = low_half((BLOCK // 2, LANES))

        def eight(j, carry):
            for i in range(SUBLANES):
                at = index * chunk + j * SUBLANES + i
                for q in range(pairs):
                    one = raw[slot, 2 * q, j, i]
                    one_turned = pltpu.roll(one, BLOCK, 1)
                    if 2 * q + 1 < slots:
                        two = raw[slot, 2 * q + 1, j, i]
                        two_turned = pltpu.roll(two, BLOCK, 1)
                    else:
                        two = two_turned = jnp.zeros_like(one)
                    both = jnp.concatenate([jnp.where(low, one, two_turned), jnp.where(low, one_turned, two)], axis=0)
                    high, rest = split(both)
                    prepared[at, :BLOCK, q * LANES : (q + 1) * LANES] = high
                    prepared[at, BLOCK:, q * LANES : (q + 1) * LANES] = rest
            return carry

        lax.fori_loop(0, chunk // SUBLANES, eight, 0)
        return carry

    def fill(k, h, indices):
        low = low_half((part, LANES))

        def one(n, carry):
            index = indices[0]
            for m, other in enumerate(indices[1:], 1):
                index = jnp.where(n == m, other, index)
            for t in range(tiles):
                x = gathered[k, h, index, :, t * LANES : (t + 1) * LANES]
                turned = pltpu.roll(x, BLOCK, 1)
                for side, value in enumerate((jnp.where(low, x, turned), jnp.where(low, turned, x))):
                    high, rest = split(value)
                    place = index * (2 * tiles) + 2 * t + side
                    blocks[place, :part, :] = high
                    blocks[place, part:, :] = rest
            return carry

        lax.fori_loop(0, len(indices), one, 0)

    def compute(k, h, first, last):
        low = low_half((part, LANES))
        low_picked = low_half((2 * part, LANES))

        def one_part(d, carry):
            target = target_of(d)

            def some_rows(step, carry):
                at = target * per_piece + step * group
                done = []
                for i in range(group):
                    base = (at + i) * slots
                    picked = [blocks[places_ref[base + s]] for s in range(slots)]
                    sides = [
                        jnp.where(low_picked, picked[2 * q], picked[2 * q + 1]) if 2 * q + 1 < slots else picked[2 * q]
                        for q in range(pairs)
                    ]
                    product = lax.dot_general(
                        jnp.concatenate(sides, axis=1),
                        prepared[at + i],
                        (((1,), (1,)), ((), ())),
                        preferred_element_type=jnp.float32,
                    )
                    total = product[:part] + product[part:]
                    done.append(total + pltpu.roll(total, BLOCK, 1))
                width = group * BLOCK
                joined = [jnp.where(low, done[2 * q], done[2 * q + 1]) for q in range(group // 2)]
                partial[k, h, target, :, pl.ds(pl.multiple_of(step * width, width), width)] = jnp.concatenate(joined, axis=1)
                return carry

            lax.fori_loop(0, per_piece // group, some_rows, 0)

            @pl.when((target != col) & at_the_end(target))
            def _():
                share_copy(k, h, target).start()

            return carry

        lax.fori_loop(first, last, one_part, 0)

    def update(k, h):
        @pl.when(col > 0)
        def _():
            share_arrival(k, h, col).wait_recv()

        @pl.when(col < n_col - 1)
        def _():
            share_arrival(k, h, n_col).wait_recv()

        here = slice(h * part, (h + 1) * part)
        lane = lax.broadcasted_iota(jnp.int32, (part, LANES), 1)
        order = lane // BLOCK * BLOCK + lane % 2 * (BLOCK // 2) + lane % BLOCK // 2

        def some(t, carry):
            for u in range(wide // LANES):
                at = pl.ds(pl.multiple_of(t * wide + u * LANES, LANES), LANES)
                total = partial[k, h, col, :, at] + landed[k, h, col, :, at] + landed[k, h, n_col, :, at]
                total = jnp.take_along_axis(total, order, axis=1)
                total = energies_ref[:, at] * terms[k][here, at] + total
                if k > 0:
                    total = 2.0 * total - terms[k - 1][here, at]
                terms[k + 1][here, at] = total
                if k + 1 < DEGREE:
                    gathered[k + 1, h, row, :, at] = total
            return carry

        lax.fori_loop(0, piece_len // wide, some, 0)

    stages = [(k, h) for k in range(DEGREE) for h in range(halves)]
    early = n_col // 2
    soon = max(n_col - 3, 0)

    for copy in fetch(0, 0):
        copy.start()
    gather_start(0, 0)

    @pl.when(col == 0)
    def _():
        landed[:, :, 0, :, :] = jnp.zeros_like(landed[:, :, 0, :, :])

    @pl.when(col == n_col - 1)
    def _():
        landed[:, :, n_col, :, :] = jnp.zeros_like(landed[:, :, n_col, :, :])

    for h in range(halves):
        gathered[0, h, row] = share_of(0, h)[...]
    lax.fori_loop(0, chunks // 2, prepare_chunk, 0)
    gather_pass(0, 0)
    for h in range(1, halves):
        gather_start(0, h)
    lax.fori_loop(chunks // 2, chunks, prepare_chunk, 0)
    gather_finish(0, 0)

    for index, (k, h) in enumerate(stages):
        later = stages[index + 1] if index + 1 < len(stages) else None
        compute(k, h, 0, early)
        if index > 0:
            update(*stages[index - 1])
            if later is not None and later[0] > 0:
                gather_start(*later)
        compute(k, h, early, n_col - 1)
        forward_some(k, h, 0, soon)
        compute(k, h, n_col - 1, n_col)
        if later is not None:
            gather_pass(*later)
        forward_some(k, h, soon, n_col - 1)
        if later is not None:
            gather_finish(*later)
    update(*stages[-1])

    for k in range(DEGREE):
        for h in range(halves):
            for copy in own_copies(k, h) + [passed_copy(k, h, d) for d in range(1, chips)]:
                copy.wait_send()
            if relay:
                for d in range(1, 3):
                    relay_copy(k, h, d).wait_send()

            def one(d, carry):
                share_copy(k, h, target_of(d)).wait_send()
                return carry

            lax.fori_loop(0, n_col - 1, one, 0)


def hand_over(filtered_ref, previous_ref, filtered_out, previous_out, sems):
    copies = [
        pltpu.make_async_copy(filtered_ref, filtered_out, sems.at[0]),
        pltpu.make_async_copy(previous_ref, previous_out, sems.at[1]),
    ]
    for copy in copies:
        copy.start()
    for copy in copies:
        copy.wait()


def shards(start_modes, energies, coupling, pattern):
    n_row, n_col = lax.axis_size("row"), lax.axis_size("col")
    modes, piece_len = start_modes.shape
    per_piece = piece_len // BLOCK
    rows, slots, entries = coupling.shape
    pairs = (slots + 1) // 2
    chunk, halves = 32, 2
    part = modes // halves
    tall = entries // LANES
    places = (pattern // per_piece // n_col * per_piece + pattern % per_piece).reshape(-1)
    by_slot = jnp.transpose(coupling, (1, 0, 2)).reshape(slots, rows // SUBLANES, SUBLANES, tall, LANES)
    vmem = pl.BlockSpec(memory_space=pltpu.VMEM)
    filtered, previous = pl.pallas_call(
        functools.partial(filter_kernel, slots, n_row, n_col, halves),
        in_specs=[pl.BlockSpec(memory_space=pltpu.SMEM), vmem, vmem, pl.BlockSpec(memory_space=pl.ANY)],
        out_specs=[vmem, vmem],
        out_shape=[jax.ShapeDtypeStruct(start_modes.shape, jnp.float32)] * 2,
        scratch_shapes=[
            pltpu.VMEM((2, slots, chunk // SUBLANES, SUBLANES, tall, LANES), jnp.float32),
            pltpu.VMEM((rows, 2 * BLOCK, pairs * LANES), jnp.bfloat16),
            pltpu.VMEM((DEGREE, halves, n_row, part, piece_len), jnp.float32),
            pltpu.VMEM((n_row * per_piece, 2 * part, LANES), jnp.bfloat16),
            pltpu.VMEM((modes, piece_len), jnp.float32),
            pltpu.VMEM((DEGREE, halves, n_col, part, piece_len), jnp.float32),
            pltpu.VMEM((DEGREE, halves, n_col + 1, part, piece_len), jnp.float32),
            pltpu.SemaphoreType.DMA((2, slots, SUBLANES)),
            pltpu.SemaphoreType.DMA((DEGREE, halves, n_row)),
            pltpu.SemaphoreType.DMA((DEGREE, halves, n_row + 1)),
            pltpu.SemaphoreType.DMA((DEGREE, halves, n_col)),
            pltpu.SemaphoreType.DMA((DEGREE, halves, n_col + 1)),
        ],
        compiler_params=pltpu.CompilerParams(collective_id=0, has_side_effects=True, vmem_limit_bytes=67043328),
        name="filter",
    )(places, start_modes, energies.reshape(1, -1), jnp.transpose(by_slot, (0, 1, 3, 2, 4)))
    anywhere = pl.BlockSpec(memory_space=pl.ANY)
    return pl.pallas_call(
        hand_over,
        in_specs=[vmem] * 2,
        out_specs=[anywhere] * 2,
        out_shape=[jax.ShapeDtypeStruct(start_modes.shape, jnp.float32)] * 2,
        scratch_shapes=[pltpu.SemaphoreType.DMA((2,))],
        name="hand_over",
    )(filtered, previous)


def solution(mesh):
    in_specs = (P(None, ("row", "col")), P(("row", "col")), P("row", "col", None), P("row", "col"))
    out_specs = (P(None, ("row", "col")), P(None, ("row", "col")))
    return jax.shard_map(shards, mesh=mesh, in_specs=in_specs, out_specs=out_specs, check_vma=False)
```

```python
import functools

import jax
import jax.numpy as jnp
from jax import lax
from jax.experimental import pallas as pl
from jax.experimental.pallas import tpu as pltpu
from jax.sharding import PartitionSpec as P

BLOCK = 64
DEGREE = 3
LANES = 128
SUBLANES = 8


def low_half(shape):
    return lax.broadcasted_iota(jnp.int32, shape, len(shape) - 1) < BLOCK


def split(x):
    high = x.astype(jnp.bfloat16)
    return high, (x - high.astype(jnp.float32)).astype(jnp.bfloat16)


MESH = pl.DeviceIdType.MESH


def schedule(n_col):
    if n_col == 4:
        return (
            ("compute", 0, 2), ("update",), ("gather",), ("forward", 0, 1), ("compute", 2, 4), ("forward", 1, 2),
            ("compute", 4, 5), ("forward", 4, 5), ("relay",), ("forward", 2, 3), ("compute", 5, 6), ("pass",),
            ("fill near",), ("forward", 5, 6), ("forward", 3, 4), ("compute", 6, 7), ("fill other",), ("far",),
            ("compute", 7, 8), ("fill far",),
        )
    others = 2 * (n_col - 1)
    return (
        ("compute", 0, 2), ("update",), ("gather",), ("compute", 2, others), ("relay",), ("pass",), ("fill near",),
        ("forward", 0, others), ("compute", others, others + 2), ("fill other",), ("far",), ("fill far",),
    )


def filter_kernel(
    slots, n_row, n_col, halves,
    places_ref, start_ref, energies_ref, coupling_ref, filtered_ref, previous_ref,
    raw, prepared, gathered, blocks, terms, partial, landed,
    raw_sem, local_sem, gather_send, gather_recv, share_send, share_recv,
):
    row, col = lax.axis_index("row"), lax.axis_index("col")
    chips = n_row // 2
    chip, core = row // 2, row % 2
    partner = chip * 2 + (1 - core)
    part, side_len = terms.shape[3:]
    tiles = side_len // LANES
    per_side = side_len // BLOCK
    per_piece = 2 * per_side
    rows = prepared.shape[0]
    group = min(16, per_side)
    pairs = (slots + 1) // 2
    stages = DEGREE * halves
    relay = chips == 4
    wide = min(side_len, 8 * LANES)

    def other_chip(d):
        if chips & (chips - 1):
            return (chip + d) % chips
        place, bit, rest = chip, 1, abs(d)
        while rest:
            if rest % 2:
                place = place + bit * (1 - 2 * (chip // bit % 2))
            bit, rest = 2 * bit, rest // 2
        return place

    def same_core(d):
        return other_chip(d) * 2 + core

    def other_core(d):
        return other_chip(d) * 2 + (1 - core)

    def mode_copies(outward, ref, degree, h, sem):
        copies = []
        for side in range(2):
            near, far = terms.at[degree, h, side], ref.at[pl.ds(h * part, part), pl.ds(side * side_len, side_len)]
            source, place = (near, far) if outward else (far, near)
            copies.append(pltpu.make_async_copy(source, place, local_sem.at[sem, h, side]))
        return copies

    chunk = raw.shape[2] * SUBLANES
    chunks = rows // chunk

    def fetch(index, slot):
        first = pl.multiple_of(index * (chunk // SUBLANES), chunk // SUBLANES)
        return [
            pltpu.make_async_copy(
                coupling_ref.at[s, pl.ds(first, chunk // SUBLANES), :, i, :],
                raw.at[slot, s, :, i],
                raw_sem.at[slot, s, i],
            )
            for s in range(slots)
            for i in range(SUBLANES)
        ]

    for h in range(halves):
        for copy in mode_copies(False, start_ref, 0, h, 0):
            copy.start()
    for copy in fetch(0, 0):
        copy.start()

    barrier = pltpu.get_barrier_semaphore()
    for d in range(1, chips):
        pl.semaphore_signal(barrier, inc=1, device_id=(same_core(d), col), device_id_type=MESH)
    pl.semaphore_signal(barrier, inc=1, device_id=(partner, col), device_id_type=MESH)
    for d in (1, n_col - 1):
        pl.semaphore_signal(barrier, inc=1, device_id=(row, (col + d) % n_col), device_id_type=MESH)

    @pl.when(col == 0)
    def _():
        landed[:, 0] = jnp.zeros_like(landed[:, 0])

    @pl.when(col == n_col - 1)
    def _():
        landed[:, n_col] = jnp.zeros_like(landed[:, n_col])

    for h in range(halves):
        for copy in mode_copies(False, start_ref, 0, h, 0):
            copy.wait()
        gathered[h, row] = terms[0, h]
    pl.semaphore_wait(barrier, chips + 2)

    def gather_copy(stage, slot, side, send, target):
        place = gathered.at[stage, slot] if side is None else gathered.at[stage, slot, side]
        return pltpu.make_async_remote_copy(
            src_ref=place,
            dst_ref=place,
            send_sem=gather_send.at[stage, send],
            recv_sem=gather_recv.at[stage, 2 * slot + (side or 0)],
            device_id=(target, col),
            device_id_type=MESH,
        )

    def own_copies(stage):
        if not relay:
            return [gather_copy(stage, row, None, d, same_core(d)) for d in range(1, chips)] + [
                gather_copy(stage, row, None, 0, partner)
            ]
        return [
            gather_copy(stage, row, 0, 0, same_core(1)),
            gather_copy(stage, row, 1, 2, same_core(2)),
            gather_copy(stage, row, 1, 1, same_core(1)),
            gather_copy(stage, row, 0, 3, same_core(2)),
            gather_copy(stage, row, None, 4, partner),
        ]

    def relay_copies(stage):
        return [
            gather_copy(stage, same_core(1), 0, 5, same_core(2)),
            gather_copy(stage, same_core(2), 1, 6, same_core(1)),
        ]

    def passed_copy(stage, d):
        return gather_copy(stage, same_core(-d), None, (6 if relay else chips) + d, partner)

    def arrival(stage, slot, side=None):
        return gather_copy(stage, slot, side, 0, partner)

    def fill(stage, indices):
        low = low_half((part, LANES))
        h = stage % halves

        def one(m, carry):
            n, side = m // 2, m % 2
            index = indices[0]
            for other, value in enumerate(indices[1:], 1):
                index = jnp.where(n == other, value, index)
            for t in range(tiles):
                x = gathered[stage, index, side, :, t * LANES : (t + 1) * LANES]
                turned = pltpu.roll(x, BLOCK, 1)
                for half, value in enumerate((jnp.where(low, x, turned), jnp.where(low, turned, x))):
                    high, rest = split(value)
                    place = index * per_piece + side * per_side + 2 * t + half
                    blocks[h, place, :part, :] = high
                    blocks[h, place, part:, :] = rest
            return carry

        lax.fori_loop(0, 2 * len(indices), one, 0)

    near = range(1, 3) if relay else range(1, chips)

    def gather_step(step, stage):
        if step == "gather":
            for copy in own_copies(stage):
                copy.start()
        elif step == "relay":
            if relay:
                for (d, side), copy in zip(((1, 0), (2, 1)), relay_copies(stage)):
                    arrival(stage, same_core(d), side).wait_recv()
                    copy.start()
        elif step == "pass":
            for d in near:
                arrival(stage, same_core(-d), 2 - d if relay else None).wait_recv()
                passed_copy(stage, d).start()
        elif step == "fill near":
            fill(stage, [row] + [same_core(-d) for d in near])
        elif step == "fill other":
            arrival(stage, partner).wait_recv()
            for d in near:
                arrival(stage, other_core(-d)).wait_recv()
            fill(stage, [partner] + [other_core(-d) for d in near])
        elif step == "far":
            if relay:
                for side in range(2):
                    arrival(stage, same_core(3), side).wait_recv()
                passed_copy(stage, 3).start()
                fill(stage, [same_core(3)])
        elif step == "fill far":
            if relay:
                arrival(stage, other_core(3)).wait_recv()
                fill(stage, [other_core(3)])

    def target_of(d):
        above, below = n_col - 1 - col, col
        lower = jnp.where(d < above, n_col - 1 - d, d - above)
        upper = jnp.where(d < below, d, n_col - 1 - (d - below))
        return jnp.where(2 * col < n_col, lower, upper)

    def share_copy(stage, target, side):
        to = jnp.where(target > col, col + 1, col - 1)
        slot = jnp.where((target < col) & (to == target), n_col, target)
        return pltpu.make_async_remote_copy(
            src_ref=partial.at[stage, target, side],
            dst_ref=landed.at[stage, slot, side],
            send_sem=share_send.at[stage, 2 * target + side],
            recv_sem=share_recv.at[stage, 2 * slot + side],
            device_id=(row, to),
            device_id_type=MESH,
        )

    def share_arrival(stage, slot, side):
        return pltpu.make_async_remote_copy(
            src_ref=partial.at[stage, 0, side],
            dst_ref=landed.at[stage, slot, side],
            send_sem=share_send.at[stage, side],
            recv_sem=share_recv.at[stage, 2 * slot + side],
            device_id=(row, (col + 1) % n_col),
            device_id_type=MESH,
        )

    def at_the_end(target):
        return jnp.where(target > col, col == 0, col == n_col - 1)

    def forward(stage, first, last):
        def one(j, carry):
            target, side = target_of(j // 2), j % 2

            @pl.when(jnp.logical_not(at_the_end(target)))
            def _():
                share_arrival(stage, target, side).wait_recv()

                def some(t, carry):
                    at = pl.ds(pl.multiple_of(t * wide, wide), wide)
                    partial[stage, target, side, :, at] = partial[stage, target, side, :, at] + landed[stage, target, side, :, at]
                    return carry

                lax.fori_loop(0, side_len // wide, some, 0)
                share_copy(stage, target, side).start()

            return carry

        lax.fori_loop(first, last, one, 0)

    def compute(stage, first, last):
        low = low_half((part, LANES))
        low_picked = low_half((2 * part, LANES))
        h = stage % halves

        def one(j, carry):
            target, side = target_of(j // 2), j % 2

            def some_rows(step, carry):
                at = target * per_piece + side * per_side + step * group
                done = []
                for i in range(group):
                    base = (at + i) * slots
                    picked = [blocks[h, places_ref[base + s]] for s in range(slots)]
                    sides = [
                        jnp.where(low_picked, picked[2 * q], picked[2 * q + 1]) if 2 * q + 1 < slots else picked[2 * q]
                        for q in range(pairs)
                    ]
                    product = lax.dot_general(
                        jnp.concatenate(sides, axis=1),
                        prepared[at + i],
                        (((1,), (1,)), ((), ())),
                        preferred_element_type=jnp.float32,
                    )
                    total = product[:part] + product[part:]
                    done.append(total + pltpu.roll(total, BLOCK, 1))
                width = group * BLOCK
                joined = [jnp.where(low, done[2 * q], done[2 * q + 1]) for q in range(group // 2)]
                there = pl.ds(pl.multiple_of(step * width, width), width)
                partial[stage, target, side, :, there] = jnp.concatenate(joined, axis=1)
                return carry

            lax.fori_loop(0, per_side // group, some_rows, 0)

            @pl.when((target != col) & at_the_end(target))
            def _():
                share_copy(stage, target, side).start()

            return carry

        lax.fori_loop(first, last, one, 0)

    def update(stage):
        k, h = stage // halves, stage % halves
        lane = lax.broadcasted_iota(jnp.int32, (part, LANES), 1)
        order = lane // BLOCK * BLOCK + lane % 2 * (BLOCK // 2) + lane % BLOCK // 2
        more = stage + halves < stages
        follower = jnp.minimum(stage + halves, stages - 1)
        before = jnp.maximum(k - 1, 0)
        for side in range(2):

            @pl.when(col > 0)
            def _():
                share_arrival(stage, col, side).wait_recv()

            @pl.when(col < n_col - 1)
            def _():
                share_arrival(stage, n_col, side).wait_recv()

            def some(t, carry):
                for u in range(wide // LANES):
                    at = pl.ds(pl.multiple_of(t * wide + u * LANES, LANES), LANES)
                    total = partial[stage, col, side, :, at] + landed[stage, col, side, :, at] + landed[stage, n_col, side, :, at]
                    total = jnp.take_along_axis(total, order, axis=1)
                    total = energies_ref[side, :, at] * terms[k, h, side, :, at] + total
                    total = jnp.where(k > 0, 2.0 * total - terms[before, h, side, :, at], total)
                    terms[k + 1, h, side, :, at] = total
                return carry

            lax.fori_loop(0, side_len // wide, some, 0)

        @pl.when(more)
        def _():
            gathered[follower, row] = terms[k + 1, h]

    def prepare_chunk(index, carry):
        slot = index % 2

        @pl.when(index + 1 < chunks)
        def _():
            for copy in fetch(index + 1, 1 - slot):
                copy.start()

        for copy in fetch(index, slot):
            copy.wait()
        low = low_half((BLOCK // 2, LANES))

        def eight(j, carry):
            for i in range(SUBLANES):
                at = index * chunk + j * SUBLANES + i
                for q in range(pairs):
                    one = raw[slot, 2 * q, j, i]
                    one_turned = pltpu.roll(one, BLOCK, 1)
                    if 2 * q + 1 < slots:
                        two = raw[slot, 2 * q + 1, j, i]
                        two_turned = pltpu.roll(two, BLOCK, 1)
                    else:
                        two = two_turned = jnp.zeros_like(one)
                    both = jnp.concatenate([jnp.where(low, one, two_turned), jnp.where(low, one_turned, two)], axis=0)
                    high, rest = split(both)
                    prepared[at, :BLOCK, q * LANES : (q + 1) * LANES] = high
                    prepared[at, BLOCK:, q * LANES : (q + 1) * LANES] = rest
            return carry

        lax.fori_loop(0, chunk // SUBLANES, eight, 0)
        return carry

    gather_step("gather", 0)
    lax.fori_loop(0, chunks // 4, prepare_chunk, 0)
    gather_step("relay", 0)
    lax.fori_loop(chunks // 4, chunks // 2, prepare_chunk, 0)
    gather_step("pass", 0)
    gather_step("fill near", 0)
    gather_step("gather", 1)
    lax.fori_loop(chunks // 2, chunks, prepare_chunk, 0)
    for step in ("fill other", "far", "fill far"):
        gather_step(step, 0)

    def one_stage(stage, carry):
        for step, *span in schedule(n_col):
            if step == "compute":
                compute(stage, *span)
            elif step == "forward":
                forward(stage, *span)
            elif step == "update":

                @pl.when(stage > 0)
                def _():
                    update(stage - 1)

            elif step == "gather":

                @pl.when((stage > 0) & (stage + 1 < stages))
                def _():
                    gather_step(step, stage + 1)

            else:

                @pl.when(stage + 1 < stages)
                def _():
                    gather_step(step, stage + 1)

        return carry

    lax.fori_loop(0, stages, one_stage, 0)
    update(stages - 1)
    outward = [(previous_ref, DEGREE - 1, 1), (filtered_ref, DEGREE, 2)]
    for ref, degree, sem in outward:
        for h in range(halves):
            for copy in mode_copies(True, ref, degree, h, sem):
                copy.start()

    def drain(stage, carry):
        for copy in own_copies(stage) + [passed_copy(stage, d) for d in range(1, chips)] + (relay_copies(stage) if relay else []):
            copy.wait_send()

        def one(j, carry):
            share_copy(stage, target_of(j // 2), j % 2).wait_send()
            return carry

        lax.fori_loop(0, 2 * (n_col - 1), one, 0)
        return carry

    lax.fori_loop(0, stages, drain, 0)
    for ref, degree, sem in outward:
        for h in range(halves):
            for copy in mode_copies(True, ref, degree, h, sem):
                copy.wait()


def hand_over(filtered_ref, previous_ref, filtered_out, previous_out, sems):
    copies = [
        pltpu.make_async_copy(filtered_ref, filtered_out, sems.at[0]),
        pltpu.make_async_copy(previous_ref, previous_out, sems.at[1]),
    ]
    for copy in copies:
        copy.start()
    for copy in copies:
        copy.wait()


def shards(start_modes, energies, coupling, pattern):
    n_row, n_col = lax.axis_size("row"), lax.axis_size("col")
    modes, piece_len = start_modes.shape
    per_piece = piece_len // BLOCK
    rows, slots, entries = coupling.shape
    pairs = (slots + 1) // 2
    chunk, halves = 16, 2
    part, side_len = modes // halves, piece_len // 2
    stages = DEGREE * halves
    tall = entries // LANES
    places = (pattern // per_piece // n_col * per_piece + pattern % per_piece).reshape(-1)
    by_slot = jnp.transpose(coupling, (1, 0, 2)).reshape(slots, rows // SUBLANES, SUBLANES, tall, LANES)
    vmem = pl.BlockSpec(memory_space=pltpu.VMEM)
    anywhere = pl.BlockSpec(memory_space=pl.ANY)
    filtered, previous = pl.pallas_call(
        functools.partial(filter_kernel, slots, n_row, n_col, halves),
        in_specs=[pl.BlockSpec(memory_space=pltpu.SMEM), anywhere, vmem, anywhere],
        out_specs=[anywhere, anywhere],
        out_shape=[jax.ShapeDtypeStruct(start_modes.shape, jnp.float32)] * 2,
        scratch_shapes=[
            pltpu.VMEM((2, slots, chunk // SUBLANES, SUBLANES, tall, LANES), jnp.float32),
            pltpu.VMEM((rows, 2 * BLOCK, pairs * LANES), jnp.bfloat16),
            pltpu.VMEM((stages, n_row, 2, part, side_len), jnp.float32),
            pltpu.VMEM((halves, n_row * per_piece, 2 * part, LANES), jnp.bfloat16),
            pltpu.VMEM((DEGREE + 1, halves, 2, part, side_len), jnp.float32),
            pltpu.VMEM((stages, n_col, 2, part, side_len), jnp.float32),
            pltpu.VMEM((stages, n_col + 1, 2, part, side_len), jnp.float32),
            pltpu.SemaphoreType.DMA((2, slots, SUBLANES)),
            pltpu.SemaphoreType.DMA((3, halves, 2)),
            pltpu.SemaphoreType.DMA((stages, max(10, n_row))),
            pltpu.SemaphoreType.DMA((stages, 2 * n_row)),
            pltpu.SemaphoreType.DMA((stages, 2 * n_col)),
            pltpu.SemaphoreType.DMA((stages, 2 * (n_col + 1))),
        ],
        compiler_params=pltpu.CompilerParams(collective_id=0, has_side_effects=True, vmem_limit_bytes=67043328),
        name="filter",
    )(places, start_modes, energies.reshape(2, 1, side_len), jnp.transpose(by_slot, (0, 1, 3, 2, 4)))
    return pl.pallas_call(
        hand_over,
        in_specs=[vmem] * 2,
        out_specs=[anywhere] * 2,
        out_shape=[jax.ShapeDtypeStruct(start_modes.shape, jnp.float32)] * 2,
        scratch_shapes=[pltpu.SemaphoreType.DMA((2,))],
        name="hand_over",
    )(filtered, previous)


def solution(mesh):
    in_specs = (P(None, ("row", "col")), P(("row", "col")), P("row", "col", None), P("row", "col"))
    out_specs = (P(None, ("row", "col")), P(None, ("row", "col")))
    return jax.shard_map(shards, mesh=mesh, in_specs=in_specs, out_specs=out_specs, check_vma=False)
```

```python
import functools

import jax
import jax.numpy as jnp
from jax import lax
from jax.experimental import pallas as pl
from jax.experimental.pallas import tpu as pltpu
from jax.sharding import PartitionSpec as P

BLOCK = 64
DEGREE = 3
LANES = 128
SUBLANES = 8


def low_half(shape):
    return lax.broadcasted_iota(jnp.int32, shape, len(shape) - 1) < BLOCK


def split(x):
    high = x.astype(jnp.bfloat16)
    return high, (x - high.astype(jnp.float32)).astype(jnp.bfloat16)


MESH = pl.DeviceIdType.MESH


def schedule(n_col):
    if n_col == 4:
        return (
            ("compute", 0, 2), ("update",), ("gather",), ("forward", 0, 1), ("compute", 2, 4), ("forward", 1, 2),
            ("compute", 4, 5), ("forward", 4, 5), ("relay",), ("forward", 2, 3), ("compute", 5, 6), ("pass",),
            ("fill near",), ("forward", 5, 6), ("forward", 3, 4), ("prepare",), ("compute", 6, 7), ("fill other",),
            ("far",), ("compute", 7, 8), ("drain",), ("fill far",),
        )
    others = 2 * (n_col - 1)
    return (
        ("compute", 0, 2), ("update",), ("gather",), ("prepare",), ("compute", 2, others), ("relay",), ("pass",), ("fill near",),
        ("forward", 0, others), ("compute", others, others + 2), ("fill other",), ("far",), ("drain",), ("fill far",),
    )


def filter_kernel(
    slots, n_row, n_col, halves,
    pattern_ref, start_ref, energies_ref, coupling_ref, filtered_ref, previous_ref,
    raw, prepared, gathered, blocks, terms, partial, landed,
    raw_sem, local_sem, gather_send, gather_recv, share_send, share_recv,
):
    row, col = lax.axis_index("row"), lax.axis_index("col")
    chips = n_row // 2
    chip, core = row // 2, row % 2
    partner = chip * 2 + (1 - core)
    part, side_len = terms.shape[3:]
    tiles = side_len // LANES
    per_side = side_len // BLOCK
    per_piece = 2 * per_side
    rows = prepared.shape[0]
    group = min(16, per_side)
    pairs = (slots + 1) // 2
    stages = DEGREE * halves
    relay = chips == 4
    wide = min(side_len, 8 * LANES)

    def other_chip(d):
        if chips & (chips - 1):
            return (chip + d) % chips
        place, bit, rest = chip, 1, abs(d)
        while rest:
            if rest % 2:
                place = place + bit * (1 - 2 * (chip // bit % 2))
            bit, rest = 2 * bit, rest // 2
        return place

    def same_core(d):
        return other_chip(d) * 2 + core

    def other_core(d):
        return other_chip(d) * 2 + (1 - core)

    def mode_copies(outward, ref, degree, h, sem):
        copies = []
        for side in range(2):
            near, far = terms.at[degree, h, side], ref.at[pl.ds(h * part, part), pl.ds(side * side_len, side_len)]
            source, place = (near, far) if outward else (far, near)
            copies.append(pltpu.make_async_copy(source, place, local_sem.at[sem, h, side]))
        return copies

    def target_of(d):
        above, below = n_col - 1 - col, col
        lower = jnp.where(d < above, n_col - 1 - d, d - above)
        upper = jnp.where(d < below, d, n_col - 1 - (d - below))
        return jnp.where(2 * col < n_col, lower, upper)

    chunk = raw.shape[2] * SUBLANES
    chunks = rows // chunk

    def first_row(index):
        per = per_piece // chunk
        return target_of(index // per) * per_piece + index % per * chunk

    def fetch(index, slot):
        first = first_row(index) // SUBLANES
        return [
            pltpu.make_async_copy(
                coupling_ref.at[s, pl.ds(first, chunk // SUBLANES), :, i, :],
                raw.at[slot, s, :, i],
                raw_sem.at[slot, s, i],
            )
            for s in range(slots)
            for i in range(SUBLANES)
        ]

    for h in range(halves):
        for copy in mode_copies(False, start_ref, 0, h, 0):
            copy.start()
    for copy in fetch(0, 0):
        copy.start()

    barrier = pltpu.get_barrier_semaphore()
    for d in range(1, chips):
        pl.semaphore_signal(barrier, inc=1, device_id=(same_core(d), col), device_id_type=MESH)
    pl.semaphore_signal(barrier, inc=1, device_id=(partner, col), device_id_type=MESH)
    for d in (1, n_col - 1):
        pl.semaphore_signal(barrier, inc=1, device_id=(row, (col + d) % n_col), device_id_type=MESH)

    @pl.when(col == 0)
    def _():
        landed[:, 0] = jnp.zeros_like(landed[:, 0])

    @pl.when(col == n_col - 1)
    def _():
        landed[:, n_col] = jnp.zeros_like(landed[:, n_col])

    for h in range(halves):
        for copy in mode_copies(False, start_ref, 0, h, 0):
            copy.wait()
        gathered[h, row] = terms[0, h]
    pl.semaphore_wait(barrier, chips + 2)

    def gather_copy(stage, slot, side, send, target):
        place = gathered.at[stage, slot] if side is None else gathered.at[stage, slot, side]
        return pltpu.make_async_remote_copy(
            src_ref=place,
            dst_ref=place,
            send_sem=gather_send.at[stage, send],
            recv_sem=gather_recv.at[stage, 2 * slot + (side or 0)],
            device_id=(target, col),
            device_id_type=MESH,
        )

    def own_copies(stage):
        if not relay:
            return [gather_copy(stage, row, None, d, same_core(d)) for d in range(1, chips)] + [
                gather_copy(stage, row, None, 0, partner)
            ]
        return [
            gather_copy(stage, row, 0, 0, same_core(1)),
            gather_copy(stage, row, 1, 2, same_core(2)),
            gather_copy(stage, row, 1, 1, same_core(1)),
            gather_copy(stage, row, 0, 3, same_core(2)),
            gather_copy(stage, row, None, 4, partner),
        ]

    def relay_copies(stage):
        return [
            gather_copy(stage, same_core(1), 0, 5, same_core(2)),
            gather_copy(stage, same_core(2), 1, 6, same_core(1)),
        ]

    def passed_copy(stage, d):
        return gather_copy(stage, same_core(-d), None, (6 if relay else chips) + d, partner)

    def arrival(stage, slot, side=None):
        return gather_copy(stage, slot, side, 0, partner)

    def fill(stage, indices):
        low = low_half((part, LANES))
        h = stage % halves

        def one(m, carry):
            n, side = m // 2, m % 2
            index = indices[0]
            for other, value in enumerate(indices[1:], 1):
                index = jnp.where(n == other, value, index)
            for t in range(tiles):
                x = gathered[stage, index, side, :, t * LANES : (t + 1) * LANES]
                turned = pltpu.roll(x, BLOCK, 1)
                for half, value in enumerate((jnp.where(low, x, turned), jnp.where(low, turned, x))):
                    high, rest = split(value)
                    place = index * per_piece + side * per_side + 2 * t + half
                    blocks[h, place, :part, :] = high
                    blocks[h, place, part:, :] = rest
            return carry

        lax.fori_loop(0, 2 * len(indices), one, 0)

    near = range(1, 3) if relay else range(1, chips)

    def gather_step(step, stage):
        if step == "gather":
            for copy in own_copies(stage):
                copy.start()
        elif step == "relay":
            if relay:
                for (d, side), copy in zip(((1, 0), (2, 1)), relay_copies(stage)):
                    arrival(stage, same_core(d), side).wait_recv()
                    copy.start()
        elif step == "pass":
            for d in near:
                arrival(stage, same_core(-d), 2 - d if relay else None).wait_recv()
                passed_copy(stage, d).start()
        elif step == "fill near":
            fill(stage, [row] + [same_core(-d) for d in near])
        elif step == "fill other":
            arrival(stage, partner).wait_recv()
            for d in near:
                arrival(stage, other_core(-d)).wait_recv()
            fill(stage, [partner] + [other_core(-d) for d in near])
        elif step == "far":
            if relay:
                for side in range(2):
                    arrival(stage, same_core(3), side).wait_recv()
                passed_copy(stage, 3).start()
                fill(stage, [same_core(3)])
        elif step == "fill far":
            if relay:
                arrival(stage, other_core(3)).wait_recv()
                fill(stage, [other_core(3)])

    def share_copy(stage, target, side):
        to = jnp.where(target > col, col + 1, col - 1)
        slot = jnp.where((target < col) & (to == target), n_col, target)
        return pltpu.make_async_remote_copy(
            src_ref=partial.at[stage, target, side],
            dst_ref=landed.at[stage, slot, side],
            send_sem=share_send.at[stage, 2 * target + side],
            recv_sem=share_recv.at[stage, 2 * slot + side],
            device_id=(row, to),
            device_id_type=MESH,
        )

    def share_arrival(stage, slot, side):
        return pltpu.make_async_remote_copy(
            src_ref=partial.at[stage, 0, side],
            dst_ref=landed.at[stage, slot, side],
            send_sem=share_send.at[stage, side],
            recv_sem=share_recv.at[stage, 2 * slot + side],
            device_id=(row, (col + 1) % n_col),
            device_id_type=MESH,
        )

    def at_the_end(target):
        return jnp.where(target > col, col == 0, col == n_col - 1)

    def forward(stage, first, last):
        def one(j, carry):
            target, side = target_of(j // 2), j % 2

            @pl.when(jnp.logical_not(at_the_end(target)))
            def _():
                share_arrival(stage, target, side).wait_recv()

                def some(t, carry):
                    at = pl.ds(pl.multiple_of(t * wide, wide), wide)
                    partial[stage, target, side, :, at] = partial[stage, target, side, :, at] + landed[stage, target, side, :, at]
                    return carry

                lax.fori_loop(0, side_len // wide, some, 0)
                share_copy(stage, target, side).start()

            return carry

        lax.fori_loop(first, last, one, 0)

    def place_of(block):
        if per_piece & (per_piece - 1) or n_col & (n_col - 1):
            return block // per_piece // n_col * per_piece + block % per_piece
        bits = per_piece.bit_length() - 1
        piece = lax.shift_right_logical(block, bits + n_col.bit_length() - 1)
        return lax.shift_left(piece, bits) + (block & (per_piece - 1))

    def compute(stage, first, last):
        low = low_half((part, LANES))
        low_picked = low_half((2 * part, LANES))
        h = stage % halves

        def one(j, carry):
            target, side = target_of(j // 2), j % 2

            def some_rows(step, carry):
                at = target * per_piece + side * per_side + step * group
                done = []
                for i in range(group):
                    picked = [blocks[h, place_of(pattern_ref[s, at + i])] for s in range(slots)]
                    sides = [
                        jnp.where(low_picked, picked[2 * q], picked[2 * q + 1]) if 2 * q + 1 < slots else picked[2 * q]
                        for q in range(pairs)
                    ]
                    product = lax.dot_general(
                        jnp.concatenate(sides, axis=1),
                        prepared[at + i],
                        (((1,), (1,)), ((), ())),
                        preferred_element_type=jnp.float32,
                    )
                    total = product[:part] + product[part:]
                    done.append(total + pltpu.roll(total, BLOCK, 1))
                width = group * BLOCK
                joined = [jnp.where(low, done[2 * q], done[2 * q + 1]) for q in range(group // 2)]
                there = pl.ds(pl.multiple_of(step * width, width), width)
                partial[stage, target, side, :, there] = jnp.concatenate(joined, axis=1)
                return carry

            lax.fori_loop(0, per_side // group, some_rows, 0)

            @pl.when((target != col) & at_the_end(target))
            def _():
                share_copy(stage, target, side).start()

            return carry

        lax.fori_loop(first, last, one, 0)

    def update(stage):
        k, h = stage // halves, stage % halves
        lane = lax.broadcasted_iota(jnp.int32, (part, LANES), 1)
        order = lane // BLOCK * BLOCK + lane % 2 * (BLOCK // 2) + lane % BLOCK // 2
        more = stage + halves < stages
        follower = jnp.minimum(stage + halves, stages - 1)
        before = jnp.maximum(k - 1, 0)
        for side in range(2):

            @pl.when(col > 0)
            def _():
                share_arrival(stage, col, side).wait_recv()

            @pl.when(col < n_col - 1)
            def _():
                share_arrival(stage, n_col, side).wait_recv()

            def some(t, carry):
                for u in range(wide // LANES):
                    at = pl.ds(pl.multiple_of(t * wide + u * LANES, LANES), LANES)
                    total = partial[stage, col, side, :, at] + landed[stage, col, side, :, at] + landed[stage, n_col, side, :, at]
                    total = jnp.take_along_axis(total, order, axis=1)
                    total = energies_ref[side, :, at] * terms[k, h, side, :, at] + total
                    total = jnp.where(k > 0, 2.0 * total - terms[before, h, side, :, at], total)
                    terms[k + 1, h, side, :, at] = total
                return carry

            lax.fori_loop(0, side_len // wide, some, 0)

        @pl.when(more)
        def _():
            gathered[follower, row] = terms[k + 1, h]

    def prepare_chunk(index, carry):
        slot = index % 2

        @pl.when(index + 1 < chunks)
        def _():
            for copy in fetch(index + 1, 1 - slot):
                copy.start()

        for copy in fetch(index, slot):
            copy.wait()
        low = low_half((BLOCK // 2, LANES))
        base = first_row(index)

        def eight(j, carry):
            for i in range(SUBLANES):
                at = base + j * SUBLANES + i
                for q in range(pairs):
                    one = raw[slot, 2 * q, j, i]
                    one_turned = pltpu.roll(one, BLOCK, 1)
                    if 2 * q + 1 < slots:
                        two = raw[slot, 2 * q + 1, j, i]
                        two_turned = pltpu.roll(two, BLOCK, 1)
                    else:
                        two = two_turned = jnp.zeros_like(one)
                    both = jnp.concatenate([jnp.where(low, one, two_turned), jnp.where(low, one_turned, two)], axis=0)
                    high, rest = split(both)
                    prepared[at, :BLOCK, q * LANES : (q + 1) * LANES] = high
                    prepared[at, BLOCK:, q * LANES : (q + 1) * LANES] = rest
            return carry

        lax.fori_loop(0, chunk // SUBLANES, eight, 0)
        return carry

    def prepare(first, last):
        lax.fori_loop(chunks * first // 16, chunks * last // 16, prepare_chunk, 0)

    gather_step("gather", 0)
    prepare(0, 5)
    gather_step("relay", 0)
    prepare(5, 9)
    gather_step("pass", 0)
    gather_step("fill near", 0)
    gather_step("gather", 1)
    prepare(9, 12)
    gather_step("fill other", 0)
    gather_step("far", 0)
    prepare(12, 14)
    gather_step("fill far", 0)

    def drain_gather(stage):
        for copy in own_copies(stage) + [passed_copy(stage, d) for d in range(1, chips)] + (relay_copies(stage) if relay else []):
            copy.wait_send()

    def drain_shares(stage):
        def one(j, carry):
            share_copy(stage, target_of(j // 2), j % 2).wait_send()
            return carry

        lax.fori_loop(0, 2 * (n_col - 1), one, 0)

    def one_stage(stage, carry):
        for step, *span in schedule(n_col):
            if step == "compute":
                compute(stage, *span)
            elif step == "forward":
                forward(stage, *span)
            elif step == "prepare":

                @pl.when(stage == 0)
                def _():
                    prepare(14, 16)

            elif step == "drain":
                drain_gather(stage)

                @pl.when(stage > 0)
                def _():
                    drain_shares(stage - 1)

            elif step == "update":

                @pl.when(stage > 0)
                def _():
                    update(stage - 1)

            elif step == "gather":

                @pl.when((stage > 0) & (stage + 1 < stages))
                def _():
                    gather_step(step, stage + 1)

            else:

                @pl.when(stage + 1 < stages)
                def _():
                    gather_step(step, stage + 1)

        return carry

    lax.fori_loop(0, stages, one_stage, 0)
    update(stages - 1)
    outward = [(previous_ref, DEGREE - 1, 1), (filtered_ref, DEGREE, 2)]
    for ref, degree, sem in outward:
        for h in range(halves):
            for copy in mode_copies(True, ref, degree, h, sem):
                copy.start()

    drain_shares(stages - 1)
    for ref, degree, sem in outward:
        for h in range(halves):
            for copy in mode_copies(True, ref, degree, h, sem):
                copy.wait()


def hand_over(filtered_ref, previous_ref, filtered_out, previous_out, held, sems):
    pieces = held.shape[1]
    tall = held.shape[2]

    def copies(inward):
        both = []
        for a, (ref, out) in enumerate(((filtered_ref, filtered_out), (previous_ref, previous_out))):
            for p in range(pieces):
                there, here = (ref if inward else out).at[pl.ds(p * tall, tall), :], held.at[a, p]
                source, place = (there, here) if inward else (here, there)
                both.append(pltpu.make_async_copy(source, place, sems.at[0 if inward else 1, a, p]))
        return both

    for copy in copies(True):
        copy.start()
    for came, goes in zip(copies(True), copies(False)):
        came.wait()
        goes.start()
    for copy in copies(False):
        copy.wait()


def shards(start_modes, energies, coupling, pattern):
    n_row, n_col = lax.axis_size("row"), lax.axis_size("col")
    modes, piece_len = start_modes.shape
    per_piece = piece_len // BLOCK
    rows, slots, entries = coupling.shape
    pairs = (slots + 1) // 2
    chunk, halves = min(16, per_piece), 2
    part, side_len = modes // halves, piece_len // 2
    stages = DEGREE * halves
    tall = entries // LANES
    by_slot = jnp.transpose(coupling, (1, 0, 2)).reshape(slots, rows // SUBLANES, SUBLANES, tall, LANES)
    vmem = pl.BlockSpec(memory_space=pltpu.VMEM)
    anywhere = pl.BlockSpec(memory_space=pl.ANY)
    filtered, previous = pl.pallas_call(
        functools.partial(filter_kernel, slots, n_row, n_col, halves),
        in_specs=[pl.BlockSpec(memory_space=pltpu.SMEM), anywhere, vmem, anywhere],
        out_specs=[anywhere, anywhere],
        out_shape=[jax.ShapeDtypeStruct(start_modes.shape, jnp.float32)] * 2,
        scratch_shapes=[
            pltpu.VMEM((2, slots, chunk // SUBLANES, SUBLANES, tall, LANES), jnp.float32),
            pltpu.VMEM((rows, 2 * BLOCK, pairs * LANES), jnp.bfloat16),
            pltpu.VMEM((stages, n_row, 2, part, side_len), jnp.float32),
            pltpu.VMEM((halves, n_row * per_piece, 2 * part, LANES), jnp.bfloat16),
            pltpu.VMEM((DEGREE + 1, halves, 2, part, side_len), jnp.float32),
            pltpu.VMEM((stages, n_col, 2, part, side_len), jnp.float32),
            pltpu.VMEM((stages, n_col + 1, 2, part, side_len), jnp.float32),
            pltpu.SemaphoreType.DMA((2, slots, SUBLANES)),
            pltpu.SemaphoreType.DMA((3, halves, 2)),
            pltpu.SemaphoreType.DMA((stages, max(10, n_row))),
            pltpu.SemaphoreType.DMA((stages, 2 * n_row)),
            pltpu.SemaphoreType.DMA((stages, 2 * n_col)),
            pltpu.SemaphoreType.DMA((stages, 2 * (n_col + 1))),
        ],
        compiler_params=pltpu.CompilerParams(collective_id=0, has_side_effects=True, vmem_limit_bytes=67043328),
        name="filter",
    )(pattern.T, start_modes, energies.reshape(2, 1, side_len), jnp.transpose(by_slot, (0, 1, 3, 2, 4)))
    return pl.pallas_call(
        hand_over,
        in_specs=[anywhere] * 2,
        out_specs=[anywhere] * 2,
        out_shape=[jax.ShapeDtypeStruct(start_modes.shape, jnp.float32)] * 2,
        scratch_shapes=[pltpu.VMEM((2, modes // SUBLANES, SUBLANES, piece_len), jnp.float32), pltpu.SemaphoreType.DMA((2, 2, modes // SUBLANES))],
        name="hand_over",
    )(filtered, previous)


def solution(mesh):
    in_specs = (P(None, ("row", "col")), P(("row", "col")), P("row", "col", None), P("row", "col"))
    out_specs = (P(None, ("row", "col")), P(None, ("row", "col")))
    return jax.shard_map(shards, mesh=mesh, in_specs=in_specs, out_specs=out_specs, check_vma=False)
```

```python
import functools

import jax
import jax.numpy as jnp
from jax import lax
from jax.experimental import pallas as pl
from jax.experimental.pallas import tpu as pltpu
from jax.sharding import PartitionSpec as P

BLOCK = 64
DEGREE = 3
LANES = 128
SUBLANES = 8


def low_half(shape):
    return lax.broadcasted_iota(jnp.int32, shape, len(shape) - 1) < BLOCK


def split(x):
    high = x.astype(jnp.bfloat16)
    return high, (x - high.astype(jnp.float32)).astype(jnp.bfloat16)


MESH = pl.DeviceIdType.MESH


def schedule(n_col):
    if n_col == 4:
        return (
            ("compute", 0, 2), ("update",), ("gather",), ("forward", 0, 1), ("compute", 2, 4), ("forward", 1, 2),
            ("compute", 4, 5), ("forward", 4, 5), ("relay",), ("forward", 2, 3), ("compute", 5, 6), ("pass",),
            ("fill near",), ("forward", 5, 6), ("forward", 3, 4), ("prepare",), ("compute", 6, 7), ("fill other",),
            ("far",), ("compute", 7, 8), ("drain",), ("fill far",),
        )
    others = 2 * (n_col - 1)
    return (
        ("compute", 0, 2), ("update",), ("gather",), ("prepare",), ("compute", 2, others), ("relay",), ("pass",), ("fill near",),
        ("forward", 0, others), ("compute", others, others + 2), ("fill other",), ("far",), ("drain",), ("fill far",),
    )


def filter_kernel(
    slots, n_row, n_col, halves,
    pattern_ref, start_ref, energies_ref, coupling_ref, filtered_ref, previous_ref,
    raw, prepared, gathered, blocks, terms, partial, landed,
    raw_sem, local_sem, gather_send, gather_recv, share_send, share_recv,
):
    row, col = lax.axis_index("row"), lax.axis_index("col")
    chips = n_row // 2
    chip, core = row // 2, row % 2
    partner = chip * 2 + (1 - core)
    part, side_len = terms.shape[3:]
    tiles = side_len // LANES
    per_side = side_len // BLOCK
    per_piece = 2 * per_side
    rows = prepared.shape[0]
    group = min(16, per_side)
    pairs = (slots + 1) // 2
    stages = DEGREE * halves
    relay = chips == 4
    near = range(1, 3) if relay else range(1, chips)
    wide = min(side_len, 8 * LANES)

    def other_chip(d):
        if chips & (chips - 1):
            return (chip + d) % chips
        place, bit, rest = chip, 1, abs(d)
        while rest:
            if rest % 2:
                place = place + bit * (1 - 2 * (chip // bit % 2))
            bit, rest = 2 * bit, rest // 2
        return place

    def same_core(d):
        return other_chip(d) * 2 + core

    def other_core(d):
        return other_chip(d) * 2 + (1 - core)

    def mode_copies(h):
        return [
            pltpu.make_async_copy(
                start_ref.at[pl.ds(h * part, part), pl.ds(side * side_len, side_len)], terms.at[0, h, side], local_sem.at[h, side]
            )
            for side in range(2)
        ]

    def target_of(d):
        above, below = n_col - 1 - col, col
        lower = jnp.where(d < above, n_col - 1 - d, d - above)
        upper = jnp.where(d < below, d, n_col - 1 - (d - below))
        return jnp.where(2 * col < n_col, lower, upper)

    ahead, chunk = raw.shape[0], raw.shape[2] * SUBLANES
    chunks = rows // chunk

    def first_row(index):
        per = per_piece // chunk
        return target_of(index // per) * per_piece + index % per * chunk

    def fetch(index, slot):
        first = first_row(index) // SUBLANES
        return [
            pltpu.make_async_copy(
                coupling_ref.at[:, pl.ds(first, chunk // SUBLANES), :, i, :],
                raw.at[slot, :, :, i],
                raw_sem.at[slot, i],
            )
            for i in range(SUBLANES)
        ]

    for h in range(halves):
        for copy in mode_copies(h):
            copy.start()
    for index in range(ahead - 1):
        for copy in fetch(index, index):
            copy.start()

    barrier = pltpu.get_barrier_semaphore()
    for d in near:
        pl.semaphore_signal(barrier, inc=1, device_id=(same_core(d), col), device_id_type=MESH)
    pl.semaphore_signal(barrier, inc=1, device_id=(partner, col), device_id_type=MESH)
    has_below, has_above = col > 0, col < n_col - 1

    @pl.when(has_below)
    def _():
        pl.semaphore_signal(barrier, inc=1, device_id=(row, col - 1), device_id_type=MESH)

    @pl.when(has_above)
    def _():
        pl.semaphore_signal(barrier, inc=1, device_id=(row, col + 1), device_id_type=MESH)

    @pl.when(col == 0)
    def _():
        landed[:, 0] = jnp.zeros_like(landed[:, 0])

    @pl.when(col == n_col - 1)
    def _():
        landed[:, n_col] = jnp.zeros_like(landed[:, n_col])

    for h in range(halves):
        for copy in mode_copies(h):
            copy.wait()
        gathered[h, row] = terms[0, h]

    def gather_copy(stage, slot, side, send, target):
        place = gathered.at[stage, slot] if side is None else gathered.at[stage, slot, side]
        return pltpu.make_async_remote_copy(
            src_ref=place,
            dst_ref=place,
            send_sem=gather_send.at[stage, send],
            recv_sem=gather_recv.at[stage, 2 * slot + (side or 0)],
            device_id=(target, col),
            device_id_type=MESH,
        )

    def own_copies(stage):
        if not relay:
            return [gather_copy(stage, row, None, d, same_core(d)) for d in range(1, chips)] + [
                gather_copy(stage, row, None, 0, partner)
            ]
        return [
            gather_copy(stage, row, 0, 0, same_core(1)),
            gather_copy(stage, row, 1, 2, same_core(2)),
            gather_copy(stage, row, 1, 1, same_core(1)),
            gather_copy(stage, row, 0, 3, same_core(2)),
            gather_copy(stage, row, None, 4, partner),
        ]

    def relay_copies(stage):
        return [
            gather_copy(stage, same_core(1), 0, 5, same_core(2)),
            gather_copy(stage, same_core(2), 1, 6, same_core(1)),
        ]

    def passed_copy(stage, d):
        return gather_copy(stage, same_core(-d), None, (6 if relay else chips) + d, partner)

    def arrival(stage, slot, side=None):
        return gather_copy(stage, slot, side, 0, partner)

    def fill(stage, indices):
        low = low_half((part, LANES))
        h = stage % halves

        def one(m, carry):
            n, side = m // 2, m % 2
            index = indices[0]
            for other, value in enumerate(indices[1:], 1):
                index = jnp.where(n == other, value, index)
            for t in range(tiles):
                x = gathered[stage, index, side, :, t * LANES : (t + 1) * LANES]
                turned = pltpu.roll(x, BLOCK, 1)
                for half, value in enumerate((jnp.where(low, x, turned), jnp.where(low, turned, x))):
                    high, rest = split(value)
                    place = index * per_piece + side * per_side + 2 * t + half
                    blocks[h, place, :part, :] = high
                    blocks[h, place, part:, :] = rest
            return carry

        lax.fori_loop(0, 2 * len(indices), one, 0)

    def gather_step(step, stage):
        if step == "gather":
            for copy in own_copies(stage):
                copy.start()
        elif step == "relay":
            if relay:
                for (d, side), copy in zip(((1, 0), (2, 1)), relay_copies(stage)):
                    arrival(stage, same_core(d), side).wait_recv()
                    copy.start()
        elif step == "pass":
            for d in near:
                arrival(stage, same_core(-d), 2 - d if relay else None).wait_recv()
                passed_copy(stage, d).start()
        elif step == "fill near":
            fill(stage, [row] + [same_core(-d) for d in near])
        elif step == "fill other":
            arrival(stage, partner).wait_recv()
            for d in near:
                arrival(stage, other_core(-d)).wait_recv()
            fill(stage, [partner] + [other_core(-d) for d in near])
        elif step == "far":
            if relay:
                for side in range(2):
                    arrival(stage, same_core(3), side).wait_recv()
                passed_copy(stage, 3).start()
                fill(stage, [same_core(3)])
        elif step == "fill far":
            if relay:
                arrival(stage, other_core(3)).wait_recv()
                fill(stage, [other_core(3)])

    def share_copy(stage, target, side):
        to = jnp.where(target > col, col + 1, col - 1)
        slot = jnp.where((target < col) & (to == target), n_col, target)
        return pltpu.make_async_remote_copy(
            src_ref=partial.at[stage, target, side],
            dst_ref=landed.at[stage, slot, side],
            send_sem=share_send.at[stage, 2 * target + side],
            recv_sem=share_recv.at[stage, 2 * slot + side],
            device_id=(row, to),
            device_id_type=MESH,
        )

    def share_arrival(stage, slot, side):
        return pltpu.make_async_remote_copy(
            src_ref=partial.at[stage, 0, side],
            dst_ref=landed.at[stage, slot, side],
            send_sem=share_send.at[stage, side],
            recv_sem=share_recv.at[stage, 2 * slot + side],
            device_id=(row, (col + 1) % n_col),
            device_id_type=MESH,
        )

    def at_the_end(target):
        return jnp.where(target > col, col == 0, col == n_col - 1)

    def forward(stage, first, last):
        def one(j, carry):
            target, side = target_of(j // 2), j % 2

            @pl.when(jnp.logical_not(at_the_end(target)))
            def _():
                share_arrival(stage, target, side).wait_recv()

                def some(t, carry):
                    at = pl.ds(pl.multiple_of(t * wide, wide), wide)
                    partial[stage, target, side, :, at] = partial[stage, target, side, :, at] + landed[stage, target, side, :, at]
                    return carry

                lax.fori_loop(0, side_len // wide, some, 0)
                share_copy(stage, target, side).start()

            return carry

        lax.fori_loop(first, last, one, 0)

    def place_of(block):
        if per_piece & (per_piece - 1) or n_col & (n_col - 1):
            return block // per_piece // n_col * per_piece + block % per_piece
        bits = per_piece.bit_length() - 1
        piece = lax.shift_right_logical(block, bits + n_col.bit_length() - 1)
        return lax.shift_left(piece, bits) + (block & (per_piece - 1))

    def compute(stage, first, last):
        low = low_half((part, LANES))
        low_picked = low_half((2 * part, LANES))
        h = stage % halves

        def one(j, carry):
            target, side = target_of(j // 2), j % 2

            def some_rows(step, carry):
                at = target * per_piece + side * per_side + step * group
                done = []
                for i in range(group):
                    picked = [blocks[h, place_of(pattern_ref[s, at + i])] for s in range(slots)]
                    sides = [
                        jnp.where(low_picked, picked[2 * q], picked[2 * q + 1]) if 2 * q + 1 < slots else picked[2 * q]
                        for q in range(pairs)
                    ]
                    product = lax.dot_general(
                        jnp.concatenate(sides, axis=1),
                        prepared[at + i],
                        (((1,), (1,)), ((), ())),
                        preferred_element_type=jnp.float32,
                    )
                    total = product[:part] + product[part:]
                    done.append(total + pltpu.roll(total, BLOCK, 1))
                width = group * BLOCK
                joined = [jnp.where(low, done[2 * q], done[2 * q + 1]) for q in range(group // 2)]
                there = pl.ds(pl.multiple_of(step * width, width), width)
                partial[stage, target, side, :, there] = jnp.concatenate(joined, axis=1)
                return carry

            lax.fori_loop(0, per_side // group, some_rows, 0)

            @pl.when((target != col) & at_the_end(target))
            def _():
                share_copy(stage, target, side).start()

            return carry

        lax.fori_loop(first, last, one, 0)

    def update(stage):
        k, h = stage // halves, stage % halves
        lane = lax.broadcasted_iota(jnp.int32, (part, LANES), 1)
        order = lane // BLOCK * BLOCK + lane % 2 * (BLOCK // 2) + lane % BLOCK // 2
        more = stage + halves < stages
        follower = jnp.minimum(stage + halves, stages - 1)
        before = jnp.maximum(k - 1, 0)
        for side in range(2):

            @pl.when(col > 0)
            def _():
                share_arrival(stage, col, side).wait_recv()

            @pl.when(col < n_col - 1)
            def _():
                share_arrival(stage, n_col, side).wait_recv()

            def some(t, carry):
                for u in range(wide // LANES):
                    at = pl.ds(pl.multiple_of(t * wide + u * LANES, LANES), LANES)
                    total = partial[stage, col, side, :, at] + landed[stage, col, side, :, at] + landed[stage, n_col, side, :, at]
                    total = jnp.take_along_axis(total, order, axis=1)
                    total = energies_ref[side, :, at] * terms[k, h, side, :, at] + total
                    total = jnp.where(k > 0, 2.0 * total - terms[before, h, side, :, at], total)
                    terms[k + 1, h, side, :, at] = total
                return carry

            lax.fori_loop(0, side_len // wide, some, 0)

        @pl.when(more)
        def _():
            gathered[follower, row] = terms[k + 1, h]

    def prepare_chunk(index, carry):
        slot = index % ahead

        @pl.when(index + ahead - 1 < chunks)
        def _():
            for copy in fetch(index + ahead - 1, (index + ahead - 1) % ahead):
                copy.start()

        for copy in fetch(index, slot):
            copy.wait()
        low = low_half((BLOCK // 2, LANES))
        base = first_row(index)

        def eight(j, carry):
            for i in range(SUBLANES):
                at = base + j * SUBLANES + i
                for q in range(pairs):
                    one = raw[slot, 2 * q, j, i]
                    one_turned = pltpu.roll(one, BLOCK, 1)
                    if 2 * q + 1 < slots:
                        two = raw[slot, 2 * q + 1, j, i]
                        two_turned = pltpu.roll(two, BLOCK, 1)
                    else:
                        two = two_turned = jnp.zeros_like(one)
                    both = jnp.concatenate([jnp.where(low, one, two_turned), jnp.where(low, one_turned, two)], axis=0)
                    high, rest = split(both)
                    prepared[at, :BLOCK, q * LANES : (q + 1) * LANES] = high
                    prepared[at, BLOCK:, q * LANES : (q + 1) * LANES] = rest
            return carry

        lax.fori_loop(0, chunk // SUBLANES, eight, 0)
        return carry

    def prepare(first, last):
        lax.fori_loop(chunks * first // 16, chunks * last // 16, prepare_chunk, 0)

    prepare(0, 3)
    beside = jnp.where(has_below, 1, 0) + jnp.where(has_above, 1, 0)
    pl.semaphore_wait(barrier, len(near) + 1 + beside)
    gather_step("gather", 0)
    prepare(3, 7)
    gather_step("relay", 0)
    prepare(7, 10)
    gather_step("pass", 0)
    gather_step("fill near", 0)
    gather_step("gather", 1)
    prepare(10, 11)
    gather_step("fill other", 0)
    gather_step("far", 0)
    prepare(11, 12)
    gather_step("fill far", 0)

    def drain_gather(stage):
        for copy in own_copies(stage) + [passed_copy(stage, d) for d in range(1, chips)] + (relay_copies(stage) if relay else []):
            copy.wait_send()

    def drain_shares(stage):
        def one(j, carry):
            share_copy(stage, target_of(j // 2), j % 2).wait_send()
            return carry

        lax.fori_loop(0, 2 * (n_col - 1), one, 0)

    def one_stage(stage, carry):
        for step, *span in schedule(n_col):
            if step == "compute":
                compute(stage, *span)
            elif step == "forward":
                forward(stage, *span)
            elif step == "prepare":

                @pl.when(stage == 0)
                def _():
                    prepare(12, 16)

            elif step == "drain":
                drain_gather(stage)

                @pl.when(stage > 0)
                def _():
                    drain_shares(stage - 1)

            elif step == "update":

                @pl.when(stage > 0)
                def _():
                    update(stage - 1)

            elif step == "gather":

                @pl.when((stage > 0) & (stage + 1 < stages))
                def _():
                    gather_step(step, stage + 1)

            else:

                @pl.when(stage + 1 < stages)
                def _():
                    gather_step(step, stage + 1)

        return carry

    lax.fori_loop(0, stages, one_stage, 0)
    update(stages - 1)
    for h in range(halves):
        for side in range(2):
            here = (slice(h * part, (h + 1) * part), slice(side * side_len, (side + 1) * side_len))
            filtered_ref[here] = terms[DEGREE, h, side]
            previous_ref[here] = terms[DEGREE - 1, h, side]
    drain_shares(stages - 1)


def shards(start_modes, energies, coupling, pattern):
    n_row, n_col = lax.axis_size("row"), lax.axis_size("col")
    modes, piece_len = start_modes.shape
    per_piece = piece_len // BLOCK
    rows, slots, entries = coupling.shape
    pairs = (slots + 1) // 2
    ahead, chunk, halves = 4, min(8, per_piece), 2
    part, side_len = modes // halves, piece_len // 2
    stages = DEGREE * halves
    tall = entries // LANES
    by_slot = jnp.transpose(coupling, (1, 0, 2)).reshape(slots, rows // SUBLANES, SUBLANES, tall, LANES)
    vmem = pl.BlockSpec(memory_space=pltpu.VMEM)
    anywhere = pl.BlockSpec(memory_space=pl.ANY)
    return pl.pallas_call(
        functools.partial(filter_kernel, slots, n_row, n_col, halves),
        in_specs=[pl.BlockSpec(memory_space=pltpu.SMEM), anywhere, vmem, anywhere],
        out_specs=[vmem, vmem],
        out_shape=[pltpu.VMEM(start_modes.shape, jnp.float32)] * 2,
        scratch_shapes=[
            pltpu.VMEM((ahead, slots, chunk // SUBLANES, SUBLANES, tall, LANES), jnp.float32),
            pltpu.VMEM((rows, 2 * BLOCK, pairs * LANES), jnp.bfloat16),
            pltpu.VMEM((stages, n_row, 2, part, side_len), jnp.float32),
            pltpu.VMEM((halves, n_row * per_piece, 2 * part, LANES), jnp.bfloat16),
            pltpu.VMEM((DEGREE + 1, halves, 2, part, side_len), jnp.float32),
            pltpu.VMEM((stages, n_col, 2, part, side_len), jnp.float32),
            pltpu.VMEM((stages, n_col + 1, 2, part, side_len), jnp.float32),
            pltpu.SemaphoreType.DMA((ahead, SUBLANES)),
            pltpu.SemaphoreType.DMA((halves, 2)),
            pltpu.SemaphoreType.DMA((stages, max(10, n_row))),
            pltpu.SemaphoreType.DMA((stages, 2 * n_row)),
            pltpu.SemaphoreType.DMA((stages, 2 * n_col)),
            pltpu.SemaphoreType.DMA((stages, 2 * (n_col + 1))),
        ],
        compiler_params=pltpu.CompilerParams(collective_id=0, has_side_effects=True, vmem_limit_bytes=65929216),
        name="filter",
    )(pattern.T, start_modes, energies.reshape(2, 1, side_len), jnp.transpose(by_slot, (0, 1, 3, 2, 4)))


def solution(mesh):
    in_specs = (P(None, ("row", "col")), P(("row", "col")), P("row", "col", None), P("row", "col"))
    out_specs = (P(None, ("row", "col")), P(None, ("row", "col")))
    return jax.shard_map(shards, mesh=mesh, in_specs=in_specs, out_specs=out_specs, check_vma=False)
```

```python
import functools

import jax
import jax.numpy as jnp
from jax import lax
from jax.experimental import pallas as pl
from jax.experimental.pallas import tpu as pltpu
from jax.sharding import PartitionSpec as P

BLOCK = 64
DEGREE = 3
LANES = 128
SUBLANES = 8


def low_half(shape):
    return lax.broadcasted_iota(jnp.int32, shape, len(shape) - 1) < BLOCK


def split(x):
    high = x.astype(jnp.bfloat16)
    return high, (x - high.astype(jnp.float32)).astype(jnp.bfloat16)


MESH = pl.DeviceIdType.MESH


def schedule(n_col):
    if n_col == 4:
        return (
            ("compute", 0, 2), ("update",), ("gather",), ("forward", 0, 1), ("compute", 2, 4), ("forward", 1, 2),
            ("compute", 4, 5), ("forward", 4, 5), ("relay",), ("forward", 2, 3), ("compute", 5, 6), ("pass",),
            ("fill near",), ("forward", 5, 6), ("forward", 3, 4), ("prepare", 14, 16), ("compute", 6, 7), ("fill other",),
            ("far",), ("compute", 7, 8), ("drain",), ("fill far",),
        )
    others = 2 * (n_col - 1)
    return (
        ("compute", 0, 2), ("update",), ("gather",), ("prepare", 14, 16), ("compute", 2, others), ("relay",), ("pass",), ("fill near",),
        ("forward", 0, others), ("compute", others, others + 2), ("fill other",), ("far",), ("drain",), ("fill far",),
    )


def filter_kernel(
    slots, n_row, n_col, halves,
    pattern_ref, start_ref, energies_ref, coupling_ref, filtered_ref, previous_ref,
    raw, prepared, gathered, blocks, terms, partial, landed,
    raw_sem, local_sem, gather_send, gather_recv, share_send, share_recv,
):
    row, col = lax.axis_index("row"), lax.axis_index("col")
    chips = n_row // 2
    chip, core = row // 2, row % 2
    partner = chip * 2 + (1 - core)
    part, side_len = terms.shape[3:]
    tiles = side_len // LANES
    per_side = side_len // BLOCK
    per_piece = 2 * per_side
    rows = prepared.shape[0]
    group = min(16, per_side)
    pairs = (slots + 1) // 2
    stages = DEGREE * halves
    relay = chips == 4
    near = range(1, 3) if relay else range(1, chips)
    wide = min(side_len, 8 * LANES)

    def other_chip(d):
        if chips & (chips - 1):
            return (chip + d) % chips
        place, bit, rest = chip, 1, abs(d)
        while rest:
            if rest % 2:
                place = place + bit * (1 - 2 * (chip // bit % 2))
            bit, rest = 2 * bit, rest // 2
        return place

    def same_core(d):
        return other_chip(d) * 2 + core

    def other_core(d):
        return other_chip(d) * 2 + (1 - core)

    def mode_copies(h):
        return [
            pltpu.make_async_copy(
                start_ref.at[pl.ds(h * part, part), pl.ds(side * side_len, side_len)], terms.at[0, h, side], local_sem.at[h, side]
            )
            for side in range(2)
        ]

    def target_of(d):
        above, below = n_col - 1 - col, col
        lower = jnp.where(d < above, n_col - 1 - d, d - above)
        upper = jnp.where(d < below, d, n_col - 1 - (d - below))
        return jnp.where(2 * col < n_col, lower, upper)

    ahead, chunk = raw.shape[0], raw.shape[2] * SUBLANES
    chunks = rows // chunk

    def first_row(index):
        per = per_piece // chunk
        return target_of(index // per) * per_piece + index % per * chunk

    def fetch(index, slot):
        first = first_row(index) // SUBLANES
        return [
            pltpu.make_async_copy(
                coupling_ref.at[:, pl.ds(first, chunk // SUBLANES), :, i, :],
                raw.at[slot, :, :, i],
                raw_sem.at[slot, i],
            )
            for i in range(SUBLANES)
        ]

    for h in range(halves):
        for copy in mode_copies(h):
            copy.start()
    for index in range(ahead - 1):
        for copy in fetch(index, index):
            copy.start()

    barrier = pltpu.get_barrier_semaphore()
    for d in near:
        pl.semaphore_signal(barrier, inc=1, device_id=(same_core(d), col), device_id_type=MESH)
    pl.semaphore_signal(barrier, inc=1, device_id=(partner, col), device_id_type=MESH)
    has_below, has_above = col > 0, col < n_col - 1

    @pl.when(has_below)
    def _():
        pl.semaphore_signal(barrier, inc=1, device_id=(row, col - 1), device_id_type=MESH)

    @pl.when(has_above)
    def _():
        pl.semaphore_signal(barrier, inc=1, device_id=(row, col + 1), device_id_type=MESH)

    @pl.when(col == 0)
    def _():
        landed[:, 0] = jnp.zeros_like(landed[:, 0])

    @pl.when(col == n_col - 1)
    def _():
        landed[:, n_col] = jnp.zeros_like(landed[:, n_col])

    for h in range(halves):
        for copy in mode_copies(h):
            copy.wait()
        gathered[h, row] = terms[0, h]

    def gather_copy(stage, slot, side, send, target):
        place = gathered.at[stage, slot] if side is None else gathered.at[stage, slot, side]
        return pltpu.make_async_remote_copy(
            src_ref=place,
            dst_ref=place,
            send_sem=gather_send.at[stage, send],
            recv_sem=gather_recv.at[stage, 2 * slot + (side or 0)],
            device_id=(target, col),
            device_id_type=MESH,
        )

    def own_copies(stage):
        if not relay:
            return [gather_copy(stage, row, None, d, same_core(d)) for d in range(1, chips)] + [
                gather_copy(stage, row, None, 0, partner)
            ]
        return [
            gather_copy(stage, row, 0, 0, same_core(1)),
            gather_copy(stage, row, 1, 2, same_core(2)),
            gather_copy(stage, row, 1, 1, same_core(1)),
            gather_copy(stage, row, 0, 3, same_core(2)),
            gather_copy(stage, row, None, 4, partner),
        ]

    def relay_copies(stage):
        return [
            gather_copy(stage, same_core(1), 0, 5, same_core(2)),
            gather_copy(stage, same_core(2), 1, 6, same_core(1)),
        ]

    def passed_copy(stage, d):
        return gather_copy(stage, same_core(-d), None, (6 if relay else chips) + d, partner)

    def arrival(stage, slot, side=None):
        return gather_copy(stage, slot, side, 0, partner)

    def fill(stage, indices):
        low = low_half((part, LANES))
        h = stage % halves

        def one(m, carry):
            n, side = m // 2, m % 2
            index = indices[0]
            for other, value in enumerate(indices[1:], 1):
                index = jnp.where(n == other, value, index)
            for t in range(tiles):
                x = gathered[stage, index, side, :, t * LANES : (t + 1) * LANES]
                turned = pltpu.roll(x, BLOCK, 1)
                for half, value in enumerate((jnp.where(low, x, turned), jnp.where(low, turned, x))):
                    high, rest = split(value)
                    place = index * per_piece + side * per_side + 2 * t + half
                    blocks[h, place, :part, :] = high
                    blocks[h, place, part:, :] = rest
            return carry

        lax.fori_loop(0, 2 * len(indices), one, 0)

    def gather_step(step, stage):
        if step == "gather":
            for copy in own_copies(stage):
                copy.start()
        elif step == "relay":
            if relay:
                for (d, side), copy in zip(((1, 0), (2, 1)), relay_copies(stage)):
                    arrival(stage, same_core(d), side).wait_recv()
                    copy.start()
        elif step == "pass":
            for d in near:
                arrival(stage, same_core(-d), 2 - d if relay else None).wait_recv()
                passed_copy(stage, d).start()
        elif step == "fill near":
            fill(stage, [row] + [same_core(-d) for d in near])
        elif step == "fill other":
            arrival(stage, partner).wait_recv()
            for d in near:
                arrival(stage, other_core(-d)).wait_recv()
            fill(stage, [partner] + [other_core(-d) for d in near])
        elif step == "far":
            if relay:
                for side in range(2):
                    arrival(stage, same_core(3), side).wait_recv()
                passed_copy(stage, 3).start()
                fill(stage, [same_core(3)])
        elif step == "fill far":
            if relay:
                arrival(stage, other_core(3)).wait_recv()
                fill(stage, [other_core(3)])

    def share_copy(stage, target, side):
        to = jnp.where(target > col, col + 1, col - 1)
        slot = jnp.where((target < col) & (to == target), n_col, target)
        return pltpu.make_async_remote_copy(
            src_ref=partial.at[stage, target, side],
            dst_ref=landed.at[stage, slot, side],
            send_sem=share_send.at[stage, 2 * target + side],
            recv_sem=share_recv.at[stage, 2 * slot + side],
            device_id=(row, to),
            device_id_type=MESH,
        )

    def share_arrival(stage, slot, side):
        return pltpu.make_async_remote_copy(
            src_ref=partial.at[stage, 0, side],
            dst_ref=landed.at[stage, slot, side],
            send_sem=share_send.at[stage, side],
            recv_sem=share_recv.at[stage, 2 * slot + side],
            device_id=(row, (col + 1) % n_col),
            device_id_type=MESH,
        )

    def at_the_end(target):
        return jnp.where(target > col, col == 0, col == n_col - 1)

    def forward(stage, first, last):
        def one(j, carry):
            target, side = target_of(j // 2), j % 2

            @pl.when(jnp.logical_not(at_the_end(target)))
            def _():
                share_arrival(stage, target, side).wait_recv()

                def some(t, carry):
                    at = pl.ds(pl.multiple_of(t * wide, wide), wide)
                    partial[stage, target, side, :, at] = partial[stage, target, side, :, at] + landed[stage, target, side, :, at]
                    return carry

                lax.fori_loop(0, side_len // wide, some, 0)
                share_copy(stage, target, side).start()

            return carry

        lax.fori_loop(first, last, one, 0)

    def place_of(block):
        if per_piece & (per_piece - 1) or n_col & (n_col - 1):
            return block // per_piece // n_col * per_piece + block % per_piece
        bits = per_piece.bit_length() - 1
        piece = lax.shift_right_logical(block, bits + n_col.bit_length() - 1)
        return lax.shift_left(piece, bits) + (block & (per_piece - 1))

    def compute(stage, first, last):
        low = low_half((part, LANES))
        low_picked = low_half((2 * part, LANES))
        h = stage % halves

        def one(j, carry):
            target, side = target_of(j // 2), j % 2

            def some_rows(step, carry):
                at = target * per_piece + side * per_side + step * group
                done = []
                for i in range(group):
                    picked = [blocks[h, place_of(pattern_ref[s, at + i])] for s in range(slots)]
                    sides = [
                        jnp.where(low_picked, picked[2 * q], picked[2 * q + 1]) if 2 * q + 1 < slots else picked[2 * q]
                        for q in range(pairs)
                    ]
                    product = lax.dot_general(
                        jnp.concatenate(sides, axis=1),
                        prepared[at + i],
                        (((1,), (1,)), ((), ())),
                        preferred_element_type=jnp.float32,
                    )
                    total = product[:part] + product[part:]
                    done.append(total + pltpu.roll(total, BLOCK, 1))
                width = group * BLOCK
                joined = [jnp.where(low, done[2 * q], done[2 * q + 1]) for q in range(group // 2)]
                there = pl.ds(pl.multiple_of(step * width, width), width)
                partial[stage, target, side, :, there] = jnp.concatenate(joined, axis=1)
                return carry

            lax.fori_loop(0, per_side // group, some_rows, 0)

            @pl.when((target != col) & at_the_end(target))
            def _():
                share_copy(stage, target, side).start()

            return carry

        lax.fori_loop(first, last, one, 0)

    def update(stage):
        k, h = stage // halves, stage % halves
        lane = lax.broadcasted_iota(jnp.int32, (part, LANES), 1)
        order = lane // BLOCK * BLOCK + lane % 2 * (BLOCK // 2) + lane % BLOCK // 2
        more = stage + halves < stages
        follower = jnp.minimum(stage + halves, stages - 1)
        before = jnp.maximum(k - 1, 0)
        for side in range(2):

            @pl.when(col > 0)
            def _():
                share_arrival(stage, col, side).wait_recv()

            @pl.when(col < n_col - 1)
            def _():
                share_arrival(stage, n_col, side).wait_recv()

            def some(t, carry):
                for u in range(wide // LANES):
                    at = pl.ds(pl.multiple_of(t * wide + u * LANES, LANES), LANES)
                    total = partial[stage, col, side, :, at] + landed[stage, col, side, :, at] + landed[stage, n_col, side, :, at]
                    total = jnp.take_along_axis(total, order, axis=1)
                    total = energies_ref[side, :, at] * terms[k, h, side, :, at] + total
                    total = jnp.where(k > 0, 2.0 * total - terms[before, h, side, :, at], total)
                    terms[k + 1, h, side, :, at] = total
                return carry

            lax.fori_loop(0, side_len // wide, some, 0)

        @pl.when(more)
        def _():
            gathered[follower, row] = terms[k + 1, h]

    def prepare_chunk(index, carry):
        slot = index % ahead

        @pl.when(index + ahead - 1 < chunks)
        def _():
            for copy in fetch(index + ahead - 1, (index + ahead - 1) % ahead):
                copy.start()

        for copy in fetch(index, slot):
            copy.wait()
        low = low_half((BLOCK // 2, LANES))
        base = first_row(index)

        def eight(j, carry):
            for i in range(SUBLANES):
                at = base + j * SUBLANES + i
                for q in range(pairs):
                    one = raw[slot, 2 * q, j, i]
                    one_turned = pltpu.roll(one, BLOCK, 1)
                    if 2 * q + 1 < slots:
                        two = raw[slot, 2 * q + 1, j, i]
                        two_turned = pltpu.roll(two, BLOCK, 1)
                    else:
                        two = two_turned = jnp.zeros_like(one)
                    both = jnp.concatenate([jnp.where(low, one, two_turned), jnp.where(low, one_turned, two)], axis=0)
                    high, rest = split(both)
                    prepared[at, :BLOCK, q * LANES : (q + 1) * LANES] = high
                    prepared[at, BLOCK:, q * LANES : (q + 1) * LANES] = rest
            return carry

        lax.fori_loop(0, chunk // SUBLANES, eight, 0)
        return carry

    def prepare(first, last):
        lax.fori_loop(chunks * first // 16, chunks * last // 16, prepare_chunk, 0)

    prepare(0, 2)
    beside = jnp.where(has_below, 1, 0) + jnp.where(has_above, 1, 0)
    pl.semaphore_wait(barrier, len(near) + 1 + beside)
    gather_step("gather", 0)
    prepare(2, 7)
    gather_step("relay", 0)
    prepare(7, 10)
    gather_step("pass", 0)
    gather_step("fill near", 0)
    gather_step("gather", 1)
    prepare(10, 12)
    gather_step("fill other", 0)
    gather_step("far", 0)
    prepare(12, 14)
    gather_step("fill far", 0)

    def drain_gather(stage):
        for copy in own_copies(stage) + [passed_copy(stage, d) for d in range(1, chips)] + (relay_copies(stage) if relay else []):
            copy.wait_send()

    def drain_shares(stage):
        def one(j, carry):
            share_copy(stage, target_of(j // 2), j % 2).wait_send()
            return carry

        lax.fori_loop(0, 2 * (n_col - 1), one, 0)

    def put_out(ref, degree, h):
        for side in range(2):
            ref[h * part : (h + 1) * part, side * side_len : (side + 1) * side_len] = terms[degree, h, side]

    def one_stage(stage, carry):
        for step, *span in schedule(n_col):
            if step == "compute":
                compute(stage, *span)
            elif step == "forward":
                forward(stage, *span)
            elif step == "prepare":

                @pl.when(stage == 0)
                def _():
                    prepare(*span)

            elif step == "drain":
                drain_gather(stage)

                @pl.when(stage == stages - 1)
                def _():
                    for h in range(halves):
                        put_out(previous_ref, DEGREE - 1, h)
                    for h in range(halves - 1):
                        put_out(filtered_ref, DEGREE, h)

                @pl.when(stage > 0)
                def _():
                    drain_shares(stage - 1)

            elif step == "update":

                @pl.when(stage > 0)
                def _():
                    update(stage - 1)

            elif step == "gather":

                @pl.when((stage > 0) & (stage + 1 < stages))
                def _():
                    gather_step(step, stage + 1)

            else:

                @pl.when(stage + 1 < stages)
                def _():
                    gather_step(step, stage + 1)

        return carry

    lax.fori_loop(0, stages, one_stage, 0)
    update(stages - 1)
    put_out(filtered_ref, DEGREE, halves - 1)
    drain_shares(stages - 1)


def shards(start_modes, energies, coupling, pattern):
    n_row, n_col = lax.axis_size("row"), lax.axis_size("col")
    modes, piece_len = start_modes.shape
    per_piece = piece_len // BLOCK
    rows, slots, entries = coupling.shape
    pairs = (slots + 1) // 2
    ahead, chunk, halves = 4, min(8, per_piece), 2
    part, side_len = modes // halves, piece_len // 2
    stages = DEGREE * halves
    tall = entries // LANES
    by_slot = jnp.transpose(coupling, (1, 0, 2)).reshape(slots, rows // SUBLANES, SUBLANES, tall, LANES)
    vmem = pl.BlockSpec(memory_space=pltpu.VMEM)
    anywhere = pl.BlockSpec(memory_space=pl.ANY)
    return pl.pallas_call(
        functools.partial(filter_kernel, slots, n_row, n_col, halves),
        in_specs=[pl.BlockSpec(memory_space=pltpu.SMEM), anywhere, vmem, anywhere],
        out_specs=[vmem, vmem],
        out_shape=[pltpu.VMEM(start_modes.shape, jnp.float32)] * 2,
        scratch_shapes=[
            pltpu.VMEM((ahead, slots, chunk // SUBLANES, SUBLANES, tall, LANES), jnp.float32),
            pltpu.VMEM((rows, 2 * BLOCK, pairs * LANES), jnp.bfloat16),
            pltpu.VMEM((stages, n_row, 2, part, side_len), jnp.float32),
            pltpu.VMEM((halves, n_row * per_piece, 2 * part, LANES), jnp.bfloat16),
            pltpu.VMEM((DEGREE + 1, halves, 2, part, side_len), jnp.float32),
            pltpu.VMEM((stages, n_col, 2, part, side_len), jnp.float32),
            pltpu.VMEM((stages, n_col + 1, 2, part, side_len), jnp.float32),
            pltpu.SemaphoreType.DMA((ahead, SUBLANES)),
            pltpu.SemaphoreType.DMA((halves, 2)),
            pltpu.SemaphoreType.DMA((stages, max(10, n_row))),
            pltpu.SemaphoreType.DMA((stages, 2 * n_row)),
            pltpu.SemaphoreType.DMA((stages, 2 * n_col)),
            pltpu.SemaphoreType.DMA((stages, 2 * (n_col + 1))),
        ],
        compiler_params=pltpu.CompilerParams(collective_id=0, has_side_effects=True, vmem_limit_bytes=65929216),
        name="filter",
    )(pattern.T, start_modes, energies.reshape(2, 1, side_len), jnp.transpose(by_slot, (0, 1, 3, 2, 4)))


def solution(mesh):
    in_specs = (P(None, ("row", "col")), P(("row", "col")), P("row", "col", None), P("row", "col"))
    out_specs = (P(None, ("row", "col")), P(None, ("row", "col")))
    return jax.shard_map(shards, mesh=mesh, in_specs=in_specs, out_specs=out_specs, check_vma=False)
```

```python
import functools

import jax
import jax.numpy as jnp
from jax import lax
from jax.experimental import pallas as pl
from jax.experimental.pallas import tpu as pltpu
from jax.sharding import PartitionSpec as P

BLOCK = 64
DEGREE = 3
LANES = 128
SUBLANES = 8


def low_half(shape):
    return lax.broadcasted_iota(jnp.int32, shape, len(shape) - 1) < BLOCK


def split(x):
    high = x.astype(jnp.bfloat16)
    return high, (x - high.astype(jnp.float32)).astype(jnp.bfloat16)


MESH = pl.DeviceIdType.MESH


def schedule(n_col):
    if n_col == 4:
        return (
            ("compute", 0, 2), ("update",), ("gather",), ("forward", 0, 1), ("compute", 2, 4), ("forward", 1, 2),
            ("compute", 4, 5), ("forward", 4, 5), ("relay",), ("forward", 2, 3), ("compute", 5, 6), ("pass",),
            ("fill near",), ("forward", 5, 6), ("forward", 3, 4), ("prepare", 14, 16), ("compute", 6, 7), ("fill other",),
            ("far",), ("compute", 7, 8), ("drain",), ("fill far",),
        )
    others = 2 * (n_col - 1)
    return (
        ("compute", 0, 2), ("update",), ("gather",), ("prepare", 14, 16), ("compute", 2, others), ("relay",), ("pass",), ("fill near",),
        ("forward", 0, others), ("compute", others, others + 2), ("fill other",), ("far",), ("drain",), ("fill far",),
    )


def filter_kernel(
    slots, n_row, n_col, halves,
    pattern_ref, start_ref, energies_ref, coupling_ref, filtered_ref, previous_ref,
    raw, prepared, gathered, blocks, terms, partial, landed,
    raw_sem, local_sem, gather_send, gather_recv, share_send, share_recv,
):
    row, col = lax.axis_index("row"), lax.axis_index("col")
    chips = n_row // 2
    chip, core = row // 2, row % 2
    partner = chip * 2 + (1 - core)
    part, side_len = terms.shape[3:]
    tiles = side_len // LANES
    per_side = side_len // BLOCK
    per_piece = 2 * per_side
    rows = prepared.shape[0]
    group = min(32, per_side)
    pairs = (slots + 1) // 2
    stages = DEGREE * halves
    relay = chips == 4
    near = range(1, 3) if relay else range(1, chips)
    wide = min(side_len, 8 * LANES)

    def other_chip(d):
        if chips & (chips - 1):
            return (chip + d) % chips
        place, bit, rest = chip, 1, abs(d)
        while rest:
            if rest % 2:
                place = place + bit * (1 - 2 * (chip // bit % 2))
            bit, rest = 2 * bit, rest // 2
        return place

    def same_core(d):
        return other_chip(d) * 2 + core

    def other_core(d):
        return other_chip(d) * 2 + (1 - core)

    def mode_copies(h):
        return [
            pltpu.make_async_copy(
                start_ref.at[pl.ds(h * part, part), pl.ds(side * side_len, side_len)], terms.at[0, h, side], local_sem.at[h, side]
            )
            for side in range(2)
        ]

    def target_of(d):
        above, below = n_col - 1 - col, col
        lower = jnp.where(d < above, n_col - 1 - d, d - above)
        upper = jnp.where(d < below, d, n_col - 1 - (d - below))
        return jnp.where(2 * col < n_col, lower, upper)

    ahead, chunk = raw.shape[0], raw.shape[2] * SUBLANES
    chunks = rows // chunk

    def first_row(index):
        per = per_piece // chunk
        return target_of(index // per) * per_piece + index % per * chunk

    def fetch(index, slot):
        first = first_row(index) // SUBLANES
        return [
            pltpu.make_async_copy(
                coupling_ref.at[:, pl.ds(first, chunk // SUBLANES), :, i, :],
                raw.at[slot, :, :, i],
                raw_sem.at[slot, i],
            )
            for i in range(SUBLANES)
        ]

    for h in range(halves):
        for copy in mode_copies(h):
            copy.start()
    for index in range(ahead - 1):
        for copy in fetch(index, index):
            copy.start()

    barrier = pltpu.get_barrier_semaphore()
    for d in near:
        pl.semaphore_signal(barrier, inc=1, device_id=(same_core(d), col), device_id_type=MESH)
    pl.semaphore_signal(barrier, inc=1, device_id=(partner, col), device_id_type=MESH)
    has_below, has_above = col > 0, col < n_col - 1

    @pl.when(has_below)
    def _():
        pl.semaphore_signal(barrier, inc=1, device_id=(row, col - 1), device_id_type=MESH)

    @pl.when(has_above)
    def _():
        pl.semaphore_signal(barrier, inc=1, device_id=(row, col + 1), device_id_type=MESH)

    @pl.when(col == 0)
    def _():
        landed[:, 0] = jnp.zeros_like(landed[:, 0])

    @pl.when(col == n_col - 1)
    def _():
        landed[:, n_col] = jnp.zeros_like(landed[:, n_col])

    for h in range(halves):
        for copy in mode_copies(h):
            copy.wait()
        gathered[h, row] = terms[0, h]

    def gather_copy(stage, slot, side, send, target):
        place = gathered.at[stage, slot] if side is None else gathered.at[stage, slot, side]
        return pltpu.make_async_remote_copy(
            src_ref=place,
            dst_ref=place,
            send_sem=gather_send.at[stage, send],
            recv_sem=gather_recv.at[stage, 2 * slot + (side or 0)],
            device_id=(target, col),
            device_id_type=MESH,
        )

    def own_copies(stage):
        if not relay:
            return [gather_copy(stage, row, None, d, same_core(d)) for d in range(1, chips)] + [
                gather_copy(stage, row, None, 0, partner)
            ]
        return [
            gather_copy(stage, row, 0, 0, same_core(1)),
            gather_copy(stage, row, 1, 2, same_core(2)),
            gather_copy(stage, row, 1, 1, same_core(1)),
            gather_copy(stage, row, 0, 3, same_core(2)),
            gather_copy(stage, row, None, 4, partner),
        ]

    def relay_copies(stage):
        return [
            gather_copy(stage, same_core(1), 0, 5, same_core(2)),
            gather_copy(stage, same_core(2), 1, 6, same_core(1)),
        ]

    def passed_copy(stage, d):
        return gather_copy(stage, same_core(-d), None, (6 if relay else chips) + d, partner)

    def arrival(stage, slot, side=None):
        return gather_copy(stage, slot, side, 0, partner)

    def fill(stage, indices):
        low = low_half((part, LANES))
        h = stage % halves

        def one(m, carry):
            n, side = m // 2, m % 2
            index = indices[0]
            for other, value in enumerate(indices[1:], 1):
                index = jnp.where(n == other, value, index)
            for t in range(tiles):
                x = gathered[stage, index, side, :, t * LANES : (t + 1) * LANES]
                turned = pltpu.roll(x, BLOCK, 1)
                for half, value in enumerate((jnp.where(low, x, turned), jnp.where(low, turned, x))):
                    high, rest = split(value)
                    place = index * per_piece + side * per_side + 2 * t + half
                    blocks[h, place, :part, :] = high
                    blocks[h, place, part:, :] = rest
            return carry

        lax.fori_loop(0, 2 * len(indices), one, 0)

    def gather_step(step, stage):
        if step == "gather":
            for copy in own_copies(stage):
                copy.start()
        elif step == "relay":
            if relay:
                for (d, side), copy in zip(((1, 0), (2, 1)), relay_copies(stage)):
                    arrival(stage, same_core(d), side).wait_recv()
                    copy.start()
        elif step == "pass":
            for d in near:
                arrival(stage, same_core(-d), 2 - d if relay else None).wait_recv()
                passed_copy(stage, d).start()
        elif step == "fill near":
            fill(stage, [row] + [same_core(-d) for d in near])
        elif step == "fill other":
            arrival(stage, partner).wait_recv()
            for d in near:
                arrival(stage, other_core(-d)).wait_recv()
            fill(stage, [partner] + [other_core(-d) for d in near])
        elif step == "far":
            if relay:
                for side in range(2):
                    arrival(stage, same_core(3), side).wait_recv()
                passed_copy(stage, 3).start()
                fill(stage, [same_core(3)])
        elif step == "fill far":
            if relay:
                arrival(stage, other_core(3)).wait_recv()
                fill(stage, [other_core(3)])

    def share_copy(stage, target, side):
        to = jnp.where(target > col, col + 1, col - 1)
        slot = jnp.where((target < col) & (to == target), n_col, target)
        return pltpu.make_async_remote_copy(
            src_ref=partial.at[stage, target, side],
            dst_ref=landed.at[stage, slot, side],
            send_sem=share_send.at[stage, 2 * target + side],
            recv_sem=share_recv.at[stage, 2 * slot + side],
            device_id=(row, to),
            device_id_type=MESH,
        )

    def share_arrival(stage, slot, side):
        return pltpu.make_async_remote_copy(
            src_ref=partial.at[stage, 0, side],
            dst_ref=landed.at[stage, slot, side],
            send_sem=share_send.at[stage, side],
            recv_sem=share_recv.at[stage, 2 * slot + side],
            device_id=(row, (col + 1) % n_col),
            device_id_type=MESH,
        )

    def at_the_end(target):
        return jnp.where(target > col, col == 0, col == n_col - 1)

    def forward(stage, first, last):
        def one(j, carry):
            target, side = target_of(j // 2), j % 2

            @pl.when(jnp.logical_not(at_the_end(target)))
            def _():
                share_arrival(stage, target, side).wait_recv()

                def some(t, carry):
                    at = pl.ds(pl.multiple_of(t * wide, wide), wide)
                    partial[stage, target, side, :, at] = partial[stage, target, side, :, at] + landed[stage, target, side, :, at]
                    return carry

                lax.fori_loop(0, side_len // wide, some, 0)
                share_copy(stage, target, side).start()

            return carry

        lax.fori_loop(first, last, one, 0)

    def place_of(block):
        if per_piece & (per_piece - 1) or n_col & (n_col - 1):
            return block // per_piece // n_col * per_piece + block % per_piece
        bits = per_piece.bit_length() - 1
        piece = lax.shift_right_logical(block, bits + n_col.bit_length() - 1)
        return lax.shift_left(piece, bits) + (block & (per_piece - 1))

    def compute(stage, first, last):
        low = low_half((part, LANES))
        low_picked = low_half((2 * part, LANES))
        h = stage % halves

        def one(j, carry):
            target, side = target_of(j // 2), j % 2

            def some_rows(step, carry):
                at = target * per_piece + side * per_side + step * group
                done = []
                for i in range(group):
                    picked = [blocks[h, place_of(pattern_ref[s, at + i])] for s in range(slots)]
                    sides = [
                        jnp.where(low_picked, picked[2 * q], picked[2 * q + 1]) if 2 * q + 1 < slots else picked[2 * q]
                        for q in range(pairs)
                    ]
                    product = lax.dot_general(
                        jnp.concatenate(sides, axis=1),
                        prepared[at + i],
                        (((1,), (1,)), ((), ())),
                        preferred_element_type=jnp.float32,
                    )
                    total = product[:part] + product[part:]
                    done.append(total + pltpu.roll(total, BLOCK, 1))
                width = group * BLOCK
                joined = [jnp.where(low, done[2 * q], done[2 * q + 1]) for q in range(group // 2)]
                there = pl.ds(pl.multiple_of(step * width, width), width)
                partial[stage, target, side, :, there] = jnp.concatenate(joined, axis=1)
                return carry

            lax.fori_loop(0, per_side // group, some_rows, 0)

            @pl.when((target != col) & at_the_end(target))
            def _():
                share_copy(stage, target, side).start()

            return carry

        lax.fori_loop(first, last, one, 0)

    def update(stage):
        k, h = stage // halves, stage % halves
        lane = lax.broadcasted_iota(jnp.int32, (part, LANES), 1)
        order = lane // BLOCK * BLOCK + lane % 2 * (BLOCK // 2) + lane % BLOCK // 2
        more = stage + halves < stages
        follower = jnp.minimum(stage + halves, stages - 1)
        before = jnp.maximum(k - 1, 0)
        for side in range(2):

            @pl.when(col > 0)
            def _():
                share_arrival(stage, col, side).wait_recv()

            @pl.when(col < n_col - 1)
            def _():
                share_arrival(stage, n_col, side).wait_recv()

            def some(t, carry):
                for u in range(wide // LANES):
                    at = pl.ds(pl.multiple_of(t * wide + u * LANES, LANES), LANES)
                    total = partial[stage, col, side, :, at] + landed[stage, col, side, :, at] + landed[stage, n_col, side, :, at]
                    total = jnp.take_along_axis(total, order, axis=1)
                    total = energies_ref[side, :, at] * terms[k, h, side, :, at] + total
                    total = jnp.where(k > 0, 2.0 * total - terms[before, h, side, :, at], total)
                    terms[k + 1, h, side, :, at] = total
                return carry

            lax.fori_loop(0, side_len // wide, some, 0)

        @pl.when(more)
        def _():
            gathered[follower, row] = terms[k + 1, h]

    def prepare_chunk(index, carry):
        slot = index % ahead

        @pl.when(index + ahead - 1 < chunks)
        def _():
            for copy in fetch(index + ahead - 1, (index + ahead - 1) % ahead):
                copy.start()

        for copy in fetch(index, slot):
            copy.wait()
        low = low_half((BLOCK // 2, LANES))
        base = first_row(index)

        def eight(j, carry):
            for i in range(SUBLANES):
                at = base + j * SUBLANES + i
                for q in range(pairs):
                    one = raw[slot, 2 * q, j, i]
                    one_turned = pltpu.roll(one, BLOCK, 1)
                    if 2 * q + 1 < slots:
                        two = raw[slot, 2 * q + 1, j, i]
                        two_turned = pltpu.roll(two, BLOCK, 1)
                    else:
                        two = two_turned = jnp.zeros_like(one)
                    both = jnp.concatenate([jnp.where(low, one, two_turned), jnp.where(low, one_turned, two)], axis=0)
                    high, rest = split(both)
                    prepared[at, :BLOCK, q * LANES : (q + 1) * LANES] = high
                    prepared[at, BLOCK:, q * LANES : (q + 1) * LANES] = rest
            return carry

        lax.fori_loop(0, chunk // SUBLANES, eight, 0)
        return carry

    def prepare(first, last):
        lax.fori_loop(chunks * first // 16, chunks * last // 16, prepare_chunk, 0)

    prepare(0, 2)
    beside = jnp.where(has_below, 1, 0) + jnp.where(has_above, 1, 0)
    pl.semaphore_wait(barrier, len(near) + 1 + beside)
    gather_step("gather", 0)
    prepare(2, 7)
    gather_step("relay", 0)
    prepare(7, 10)
    gather_step("pass", 0)
    gather_step("fill near", 0)
    gather_step("gather", 1)
    prepare(10, 12)
    gather_step("fill other", 0)
    gather_step("far", 0)
    prepare(12, 14)
    gather_step("fill far", 0)

    def drain_gather(stage):
        for copy in own_copies(stage) + [passed_copy(stage, d) for d in range(1, chips)] + (relay_copies(stage) if relay else []):
            copy.wait_send()

    def drain_shares(stage):
        def one(j, carry):
            share_copy(stage, target_of(j // 2), j % 2).wait_send()
            return carry

        lax.fori_loop(0, 2 * (n_col - 1), one, 0)

    def put_out(ref, degree, h):
        for side in range(2):
            ref[h * part : (h + 1) * part, side * side_len : (side + 1) * side_len] = terms[degree, h, side]

    def one_stage(stage, carry):
        for step, *span in schedule(n_col):
            if step == "compute":
                compute(stage, *span)
            elif step == "forward":
                forward(stage, *span)
            elif step == "prepare":

                @pl.when(stage == 0)
                def _():
                    prepare(*span)

            elif step == "drain":
                drain_gather(stage)

                @pl.when(stage == stages - 1)
                def _():
                    for h in range(halves):
                        put_out(previous_ref, DEGREE - 1, h)
                    for h in range(halves - 1):
                        put_out(filtered_ref, DEGREE, h)

                @pl.when(stage > 0)
                def _():
                    drain_shares(stage - 1)

            elif step == "update":

                @pl.when(stage > 0)
                def _():
                    update(stage - 1)

            elif step == "gather":

                @pl.when((stage > 0) & (stage + 1 < stages))
                def _():
                    gather_step(step, stage + 1)

            else:

                @pl.when(stage + 1 < stages)
                def _():
                    gather_step(step, stage + 1)

        return carry

    lax.fori_loop(0, stages, one_stage, 0)
    update(stages - 1)
    put_out(filtered_ref, DEGREE, halves - 1)
    drain_shares(stages - 1)


def shards(start_modes, energies, coupling, pattern):
    n_row, n_col = lax.axis_size("row"), lax.axis_size("col")
    modes, piece_len = start_modes.shape
    per_piece = piece_len // BLOCK
    rows, slots, entries = coupling.shape
    pairs = (slots + 1) // 2
    ahead, chunk, halves = 4, min(8, per_piece), 2
    part, side_len = modes // halves, piece_len // 2
    stages = DEGREE * halves
    tall = entries // LANES
    by_slot = jnp.transpose(coupling, (1, 0, 2)).reshape(slots, rows // SUBLANES, SUBLANES, tall, LANES)
    vmem = pl.BlockSpec(memory_space=pltpu.VMEM)
    anywhere = pl.BlockSpec(memory_space=pl.ANY)
    return pl.pallas_call(
        functools.partial(filter_kernel, slots, n_row, n_col, halves),
        in_specs=[pl.BlockSpec(memory_space=pltpu.SMEM), anywhere, vmem, anywhere],
        out_specs=[vmem, vmem],
        out_shape=[pltpu.VMEM(start_modes.shape, jnp.float32)] * 2,
        scratch_shapes=[
            pltpu.VMEM((ahead, slots, chunk // SUBLANES, SUBLANES, tall, LANES), jnp.float32),
            pltpu.VMEM((rows, 2 * BLOCK, pairs * LANES), jnp.bfloat16),
            pltpu.VMEM((stages, n_row, 2, part, side_len), jnp.float32),
            pltpu.VMEM((halves, n_row * per_piece, 2 * part, LANES), jnp.bfloat16),
            pltpu.VMEM((DEGREE + 1, halves, 2, part, side_len), jnp.float32),
            pltpu.VMEM((stages, n_col, 2, part, side_len), jnp.float32),
            pltpu.VMEM((stages, n_col + 1, 2, part, side_len), jnp.float32),
            pltpu.SemaphoreType.DMA((ahead, SUBLANES)),
            pltpu.SemaphoreType.DMA((halves, 2)),
            pltpu.SemaphoreType.DMA((stages, max(10, n_row))),
            pltpu.SemaphoreType.DMA((stages, 2 * n_row)),
            pltpu.SemaphoreType.DMA((stages, 2 * n_col)),
            pltpu.SemaphoreType.DMA((stages, 2 * (n_col + 1))),
        ],
        compiler_params=pltpu.CompilerParams(collective_id=0, has_side_effects=True, vmem_limit_bytes=65929216),
        name="filter",
    )(pattern.T, start_modes, energies.reshape(2, 1, side_len), jnp.transpose(by_slot, (0, 1, 3, 2, 4)))


def solution(mesh):
    in_specs = (P(None, ("row", "col")), P(("row", "col")), P("row", "col", None), P("row", "col"))
    out_specs = (P(None, ("row", "col")), P(None, ("row", "col")))
    return jax.shard_map(shards, mesh=mesh, in_specs=in_specs, out_specs=out_specs, check_vma=False)
```
